32 devices in a mesh: row: 4 (over z), col: 4 (over y, x), rep: 2 (over core).
Axes of the slice: x: 2, y: 2, z: 4, core: 2. Of those that a mesh axis runs over, the one named last changes fastest.
Arguments:
- features: bfloat16 [4096, 512], P(('row', 'col', 'rep')), may hold values from -6 to 6
- w_self: bfloat16 [512, 512], replicated, may hold values from -0.25 to 0.25
- w_neigh: bfloat16 [512, 512], replicated, may hold values from -1.0546875 to 1.0546875
- cotangent: bfloat16 [4096, 512], P(('row', 'col', 'rep')), may hold values from -6 to 6
- tile_row: int32 [2560], P(('row', 'col', 'rep')), may hold values from 0 to 7
- tile_col: int32 [2560], P(('row', 'col', 'rep')), may hold values from 0 to 7
- tile_mask: int32 [2560, 128, 128], P(('row', 'col', 'rep')), may hold values from 0 to 1
- tile_count: int32 [32], P(('row', 'col', 'rep')), may hold values from 20 to 80, as said below
Outputs:
- activated: bfloat16 [4096, 512], P(('row', 'col', 'rep'))
- grad_features: bfloat16 [4096, 512], P(('row', 'col', 'rep'))
- grad_weights: float32 [1024, 512], P(('row', 'col', 'rep'))
The draws below stay inside these ranges and needn't reach their ends.
Inputs may be any that keep to these rules, and one draw needn't show every extreme that they name: `tile_count`: slots below a device's count hold its live tiles; the others are ignored. Some device's count is 80.
All inputs are finite; a program needn't handle non-finite values.
Results may differ from the reference program's by a relative error of at most 0.0055.
Values may be sent and summed in bfloat16 or wider, within the bound.
A program may use at most 128 MiB of HBM per device.

```python
import math
import jax
import jax.numpy as jnp
from jax import lax

D = 512
TILE = 128
SLOTS = 80
ROW_BLOCKS = 8
COL_BLOCKS = 8
NDEV = 32
NODES = 4096
N_ROW = 4
N_COL = 4
N_REP = 2


def draw_tile_count(key, part):
    first_key, second_key = jax.random.split(key)
    total_devices = N_ROW * N_COL * N_REP
    counts = jax.random.randint(first_key, (total_devices,), SLOTS // 4, SLOTS + 1, dtype=jnp.int32)
    chosen = jax.random.randint(second_key, (), 0, total_devices, dtype=jnp.int32)
    return jnp.where(jnp.arange(total_devices, dtype=jnp.int32) == chosen, SLOTS, counts).astype(jnp.int32)


def draw_tile_mask(key, part):
    first_key, second_key = jax.random.split(key)
    total_slots = N_ROW * N_COL * N_REP * SLOTS
    groups = N_COL * N_REP
    slot_group = jnp.arange(total_slots, dtype=jnp.int32) // SLOTS % groups
    density = 2 + 4 * slot_group // max(groups - 1, 1)
    row_factor = jax.random.randint(first_key, (total_slots, TILE, 1), 1, 4, dtype=jnp.int32)
    raw_values = jax.random.randint(second_key, (total_slots, TILE, TILE), 0, 8 * TILE, dtype=jnp.int32)
    return (raw_values < density[:, None, None] * row_factor).astype(jnp.int32)


def plant(entries, key, low, top_value):
    extent = entries.shape
    index_at = [jax.random.randint(jax.random.fold_in(key, axis), (), 0, extent[axis]) for axis in range(len(extent))]
    entries = entries.at[tuple(index_at)].set(low)
    longest = extent.index(max(extent))
    index_at[longest] = (index_at[longest] + 1) % extent[longest]
    return entries.at[tuple(index_at)].set(top_value)


def level_of(stream_key, shape, shards, low, top_value):
    def one(dim, blocks):
        draws = jax.random.uniform(jax.random.fold_in(jax.random.fold_in(stream_key, 6), dim), (blocks,), jnp.float32, low / len(shards), top_value / len(shards))
        return jnp.repeat(jnp.exp(draws), shape[dim] // blocks).reshape((-1,) + (1,) * (len(shape) - dim - 1))

    level = one(*shards[0])
    for cut in shards[1:]:
        level = level * one(*cut)
    return level


def scatter_about(rng, extent, width, bound, pieces=(), held_as=jnp.bfloat16):
    drawn = jax.random.normal(rng, extent, jnp.float32) * width
    if len(pieces) > 0:
        drawn = level_of(rng, extent, pieces, -0.22, 0.18) * drawn
    return jnp.clip(drawn, min=-bound, max=bound).astype(held_as)


def setup_inputs(seed: int = 0) -> dict:
    streams_of = jax.random.split(jax.random.key(seed), 9)
    features = scatter_about(streams_of[0], (NODES, D), 1.0, 6.0, ((0, 32),))
    w_self = scatter_about(streams_of[1], (D, D), D ** -0.5, 0.25)
    w_neigh = scatter_about(streams_of[2], (D, D), (4 * D ** -0.5), 1.0546875)
    cotangent = scatter_about(streams_of[3], (NODES, D), 1.0, 6.0, ((0, 32),))
    tile_row = plant(jax.random.randint(streams_of[4], (NDEV * SLOTS,), 0, ROW_BLOCKS), jax.random.fold_in(streams_of[4], 1), 0, ROW_BLOCKS - 1).astype(jnp.int32)
    tile_col = plant(jax.random.randint(streams_of[5], (NDEV * SLOTS,), 0, COL_BLOCKS), jax.random.fold_in(streams_of[5], 1), 0, COL_BLOCKS - 1).astype(jnp.int32)
    tile_mask = draw_tile_mask(jax.random.fold_in(streams_of[8], 71), 0)
    tile_count = draw_tile_count(jax.random.fold_in(streams_of[8], 71), 0)
    return dict(features=features, w_self=w_self, w_neigh=w_neigh, cotangent=cotangent, tile_row=tile_row, tile_col=tile_col, tile_mask=tile_mask, tile_count=tile_count)


HIGHEST_PRECISION = lax.Precision.HIGHEST

def device_tiles(device, tile_row, tile_col, tile_mask, tile_count):
    slot_ids = jnp.arange(SLOTS, dtype=jnp.int32)
    first_slot = (device * SLOTS).astype(jnp.int32)
    row_ids = lax.dynamic_slice_in_dim(tile_row, first_slot, SLOTS)
    col_ids = lax.dynamic_slice_in_dim(tile_col, first_slot, SLOTS)
    tile_masks = lax.dynamic_slice_in_dim(tile_mask, first_slot, SLOTS, 0)
    live_slots = (slot_ids < tile_count[device]).astype(jnp.float32)
    tile_weights = tile_masks.astype(jnp.float32) * live_slots[:, None, None]
    row_owner = device // ROW_BLOCKS
    col_owner = device // N_REP % N_COL
    dest_blocks = (row_owner * ROW_BLOCKS + row_ids).astype(jnp.int32)
    source_blocks = (col_ids // N_REP * ROW_BLOCKS + col_owner * N_REP + col_ids % N_REP).astype(jnp.int32)
    return (dest_blocks, source_blocks, tile_weights)

def reference(features, w_self, w_neigh, cotangent, tile_row, tile_col, tile_mask, tile_count):
    feature_blocks = features.reshape(NDEV, TILE, D).astype(jnp.float32)
    device_ids = jnp.arange(NDEV, dtype=jnp.int32)

    def gather_step(carry, device):
        totals, degree = carry
        dest_blocks, source_blocks, tile_weights = device_tiles(device, tile_row, tile_col, tile_mask, tile_count)
        product = jnp.einsum('tij,tjd->tid', tile_weights, feature_blocks[source_blocks], precision=HIGHEST_PRECISION)
        totals = totals.at[dest_blocks].add(product)
        degree = degree.at[dest_blocks].add(lax.optimization_barrier(jnp.sum(tile_weights, axis=2)))
        return ((totals, degree), None)
    initial = (jnp.zeros((NDEV, TILE, D), jnp.float32), jnp.zeros((NDEV, TILE), jnp.float32))
    (totals, degree), unused = lax.scan(gather_step, initial, device_ids)
    divisor = degree.reshape(NODES, 1) + 1.0
    aggregate = (totals.reshape(NODES, D) / divisor).astype(jnp.bfloat16)
    preact = jnp.dot(features, w_self, preferred_element_type=jnp.float32) + jnp.dot(aggregate, w_neigh, preferred_element_type=jnp.float32)
    activated, pullback = jax.vjp(lambda value: jax.nn.gelu(value, approximate=True), preact)
    pre_grad = pullback(cotangent.astype(jnp.float32))[0].astype(jnp.bfloat16)
    inv_root = 1.0 / math.sqrt(NODES)
    grad_weights = jnp.concatenate([jnp.dot(features.T, pre_grad, preferred_element_type=jnp.float32), jnp.dot(aggregate.T, pre_grad, preferred_element_type=jnp.float32)], axis=0) * inv_root
    neighbour_grad = (jnp.dot(pre_grad, w_neigh.T, preferred_element_type=jnp.float32) / divisor).astype(jnp.bfloat16)
    grad_blocks = neighbour_grad.reshape(NDEV, TILE, D).astype(jnp.float32)

    def spread_step(spread, device):
        dest_blocks, source_blocks, tile_weights = device_tiles(device, tile_row, tile_col, tile_mask, tile_count)
        product = jnp.einsum('tij,tid->tjd', tile_weights, grad_blocks[dest_blocks], precision=HIGHEST_PRECISION)
        return (spread.at[source_blocks].add(product), None)
    spread, unused = lax.scan(spread_step, jnp.zeros((NDEV, TILE, D), jnp.float32), device_ids)
    grad_features = (jnp.dot(pre_grad, w_self.T, preferred_element_type=jnp.float32) + spread.reshape(NODES, D)).astype(jnp.bfloat16)
    return (activated.astype(jnp.bfloat16), grad_features, grad_weights)
```

```python
import math

import jax
import jax.numpy as jnp
from jax import lax
from jax.experimental import pallas as pl
from jax.experimental.pallas import tpu as pltpu
from jax.sharding import PartitionSpec as P


def build_kernel(group, tile, rows_ref, cols_ref, count_ref, mask_ref, adj_ref):
    step = pl.program_id(0)

    @pl.when(step == 0)
    def _():
        adj_ref[...] = jnp.zeros_like(adj_ref)

    for lane in range(group):
        slot = step * group + lane

        @pl.when(slot < count_ref[0])
        def _():
            row = pl.multiple_of(rows_ref[slot] * tile, tile)
            col = pl.multiple_of(cols_ref[slot] * tile, tile)
            where = (pl.ds(row, tile), pl.ds(col, tile))
            adj_ref[where] += mask_ref[lane].astype(jnp.float32).astype(jnp.bfloat16)


def build_adjacency(tile_row, tile_col, tile_count, tile_mask, row_blocks, col_blocks):
    slots, tile, _ = tile_mask.shape
    group = math.gcd(slots, 8)
    shape = (row_blocks * tile, col_blocks * tile)
    return pl.pallas_call(
        lambda *refs: build_kernel(group, tile, *refs),
        out_shape=jax.ShapeDtypeStruct(shape, jnp.bfloat16),
        grid_spec=pltpu.PrefetchScalarGridSpec(
            num_scalar_prefetch=3,
            grid=(slots // group,),
            in_specs=[pl.BlockSpec((group, tile, tile), lambda step, *_: (step, 0, 0))],
            out_specs=pl.BlockSpec(shape, lambda step, *_: (0, 0)),
        ),
        compiler_params=pltpu.CompilerParams(vmem_limit_bytes=48 * 2**20),
        cost_estimate=pl.CostEstimate(
            flops=slots * tile * tile, bytes_accessed=slots * tile * tile * 4, transcendentals=0
        ),
    )(tile_row, tile_col, tile_count, tile_mask)


def shards(features, w_self, w_neigh, cotangent, tile_row, tile_col, tile_mask, tile_count):
    row_devices = lax.axis_size("row")
    col_devices = lax.axis_size("col")
    rep_devices = lax.axis_size("rep")
    device_total = row_devices * col_devices * rep_devices
    tile_size = features.shape[0]
    row_blocks = col_devices * rep_devices
    col_blocks = row_devices * rep_devices
    gathered = lax.all_gather(features, ("row", "rep"), axis=0, tiled=True)
    adjacency = build_adjacency(tile_row, tile_col, tile_count, tile_mask, row_blocks, col_blocks)
    totals = jnp.dot(adjacency, gathered, preferred_element_type=jnp.float32)
    degree = jnp.sum(adjacency.astype(jnp.float32), axis=1)
    own_sum, own_degree = (
        lax.psum_scatter(totals, ("col", "rep"), scatter_dimension=0, tiled=True),
        lax.psum_scatter(degree, ("col", "rep"), scatter_dimension=0, tiled=True),
    )
    divisor = own_degree[:, None] + 1.0
    aggregate = (own_sum / divisor).astype(jnp.bfloat16)
    preact = jnp.dot(features, w_self, preferred_element_type=jnp.float32) + jnp.dot(
        aggregate, w_neigh, preferred_element_type=jnp.float32
    )
    activated, pullback = jax.vjp(lambda value: jax.nn.gelu(value, approximate=True), preact)
    pre_grad = pullback(cotangent.astype(jnp.float32))[0].astype(jnp.bfloat16)
    inv_root = 1.0 / math.sqrt(tile_size * device_total)
    local_grads = (
        jnp.concatenate(
            [
                jnp.dot(features.T, pre_grad, preferred_element_type=jnp.float32),
                jnp.dot(aggregate.T, pre_grad, preferred_element_type=jnp.float32),
            ],
            axis=0,
        )
        * inv_root
    )
    neighbour_grad = (
        jnp.dot(pre_grad, w_neigh.T, preferred_element_type=jnp.float32) / divisor
    ).astype(jnp.bfloat16)
    slab_grads = lax.all_gather(neighbour_grad, ("col", "rep"), axis=0, tiled=True)
    grad_weights = lax.psum_scatter(
        local_grads, ("row", "col", "rep"), scatter_dimension=0, tiled=True
    )
    spread = lax.dot_general(
        adjacency, slab_grads, (((0,), (0,)), ((), ())), preferred_element_type=jnp.float32
    )
    returned = lax.psum_scatter(spread, ("row", "rep"), scatter_dimension=0, tiled=True)
    grad_features = (
        jnp.dot(pre_grad, w_self.T, preferred_element_type=jnp.float32) + returned
    ).astype(jnp.bfloat16)
    return (activated.astype(jnp.bfloat16), grad_features, grad_weights)


def solution(mesh):
    placed = (
        P(("row", "col", "rep"), None),
        P(),
        P(),
        P(("row", "col", "rep"), None),
        P(("row", "col", "rep")),
        P(("row", "col", "rep")),
        P(("row", "col", "rep"), None, None),
        P(("row", "col", "rep")),
    )
    return jax.shard_map(
        shards,
        mesh=mesh,
        in_specs=placed,
        out_specs=(
            P(("row", "col", "rep"), None),
            P(("row", "col", "rep"), None),
            P(("row", "col", "rep"), None),
        ),
        check_vma=False,
    )
```

```python
import functools
import math

import jax
import jax.numpy as jnp
from jax import lax
from jax.experimental import pallas as pl
from jax.experimental.pallas import tpu as pltpu
from jax.sharding import PartitionSpec as P


def build_kernel(group, tile, row_blocks, rows_ref, cols_ref, count_ref, mask_ref, adj_ref):
    step = pl.program_id(0)

    @pl.when(step == 0)
    def _():
        adj_ref[...] = jnp.zeros_like(adj_ref)

    for lane in range(group):
        slot = step * group + lane

        @pl.when(slot < count_ref[0])
        def _():
            dest = rows_ref[slot]
            place = dest % 2 * (row_blocks // 2) + dest // 2
            row = pl.multiple_of(place * tile, tile)
            col = pl.multiple_of(cols_ref[slot] * tile, tile)
            where = (pl.ds(row, tile), pl.ds(col, tile))
            adj_ref[where] += mask_ref[lane].astype(jnp.float32).astype(jnp.bfloat16)


def build_adjacency(tile_row, tile_col, tile_count, tile_mask, row_blocks, col_blocks):
    slots, tile, _ = tile_mask.shape
    group = math.gcd(slots, 8)
    shape = (row_blocks * tile, col_blocks * tile)
    return pl.pallas_call(
        lambda *refs: build_kernel(group, tile, row_blocks, *refs),
        out_shape=jax.ShapeDtypeStruct(shape, jnp.bfloat16),
        grid_spec=pltpu.PrefetchScalarGridSpec(
            num_scalar_prefetch=3,
            grid=(slots // group,),
            in_specs=[pl.BlockSpec((group, tile, tile), lambda step, *_: (step, 0, 0))],
            out_specs=pl.BlockSpec(shape, lambda step, *_: (0, 0)),
        ),
        compiler_params=pltpu.CompilerParams(vmem_limit_bytes=48 * 2**20),
        cost_estimate=pl.CostEstimate(
            flops=slots * tile * tile, bytes_accessed=slots * tile * tile * 4, transcendentals=0
        ),
    )(tile_row, tile_col, tile_count, tile_mask)


MESH = pl.DeviceIdType.MESH
F32 = jnp.float32
BF16 = jnp.bfloat16


def each(start, stop, body):
    if stop - start <= 8:
        for k in range(start, stop):
            body(k)
    else:

        def step(k, carry):
            body(k)
            return carry

        lax.fori_loop(start, stop, step, 0)


def mm(a, b, dims=((1,), (0,))):
    return lax.dot_general(a, b, (dims, ((), ())), preferred_element_type=F32)


def layer_kernel(R, C, m, inv_root, adj, feat, ws, wn, cot, act_out, gf_out, gw_out, *scratch):
    (
        asib, xg, deg_send, deg_recv, sum_send, sum_recv, own_sum, self_pre, agg_ref, pre_ref,
        ngs, sp_sib_send, sp_sib_recv, sp_recv, sp_own, gw_send, gw_sib, gw1_send,
        gw1_recv, gw_tot, gw2_send, gw2_recv, sib_sems, row_sems, fwd_sems, deg_sems, sum_sems,
        ng_sems, sps_sems, sp_sems, gw1_sems, gw2_sems,
    ) = scratch
    T, D = feat.shape
    r, c, p = lax.axis_index("row"), lax.axis_index("col"), lax.axis_index("rep")
    q = 1 - p
    barrier = pltpu.get_barrier_semaphore()
    pl.semaphore_signal(barrier, inc=1, device_id={"rep": q}, device_id_type=MESH)
    each(1, R, lambda k: pl.semaphore_signal(
        barrier, inc=1, device_id={"row": lax.rem(r + k, R)}, device_id_type=MESH))
    each(1, C, lambda k: pl.semaphore_signal(
        barrier, inc=1, device_id={"col": lax.rem(c + k, C)}, device_id_type=MESH))
    pl.semaphore_wait(barrier, R + C - 1)

    def remote(src, dst, sems, k, target):
        return pltpu.make_async_remote_copy(
            src_ref=src, dst_ref=dst, send_sem=sems.at[0, k], recv_sem=sems.at[1, k],
            device_id=target, device_id_type=MESH)

    def row_to(k):
        return {"row": lax.rem(r + k, R)}

    def col_to(k):
        return {"col": lax.rem(c + k, C)}

    sib = {"rep": q}
    mine = r * 2 + p

    def feat_copy(k):
        return remote(feat, xg.at[mine], row_sems, k, row_to(k))

    def fwd_copy(k):
        block = lax.rem(r + R - k, R) * 2 + p
        source = feat if isinstance(k, int) and k == 0 else xg.at[block]
        return remote(source, xg.at[block], fwd_sems, k, sib)

    each(1, R, lambda k: feat_copy(k).start())
    adj_copy = remote(adj.at[q], asib, sib_sems, 0, sib)
    adj_copy.start()
    fwd_copy(0).start()
    xg[mine] = feat[...]
    self_pre[...] = mm(feat[...], ws[...])

    adj_copy.wait()
    asib[...] += adj[p]

    def rows_of(block):
        return asib[pl.ds(pl.multiple_of(block * T, T), T), :]

    ones = jnp.ones((8, asib.shape[1]), BF16)

    def deg_copy(k):
        return remote(deg_send.at[k], deg_recv.at[k], deg_sems, k, col_to(k))

    def send_degree(k):
        deg_send[k] = mm(ones, rows_of(lax.rem(c + k, C)), ((1,), (1,)))
        deg_copy(k).start()

    each(1, C, send_degree)
    degree = mm(ones, rows_of(c), ((1,), (1,)))

    def forward(k):
        feat_copy(k).wait_recv()
        fwd_copy(k).start()

    each(1, R, forward)
    each(0, R, lambda k: fwd_copy(k).wait_recv())
    sources = xg[...].reshape(R * 2 * T, D)

    def sum_copy(k):
        return remote(sum_send.at[k], sum_recv.at[k], sum_sems, k, col_to(k))

    def send_sum(k):
        sum_send[k] = mm(rows_of(lax.rem(c + k, C)), sources).astype(BF16)
        sum_copy(k).start()

    each(1, C, send_sum)
    own_sum[...] = mm(rows_of(c), sources)
    for k in range(1, C):
        deg_copy(k).wait_recv()
        degree = degree + deg_recv[k]
    diagonal = lax.broadcasted_iota(jnp.int32, (T, T), 0) == lax.broadcasted_iota(
        jnp.int32, (T, T), 1)
    spread_degree = jnp.broadcast_to(degree[0:1, :], (T, T))
    divisor = jnp.sum(jnp.where(diagonal, spread_degree, 0.0), axis=1, keepdims=True) + 1.0
    total = own_sum[...]
    for k in range(1, C):
        sum_copy(k).wait_recv()
        total = total + sum_recv[k].astype(F32)
    aggregate = (total / divisor).astype(BF16)
    v = self_pre[...] + mm(aggregate, wn[...])
    root = math.sqrt(2.0 / math.pi)
    t = jnp.tanh(root * (v + 0.044715 * (v * v * v)))
    slope = 0.5 * (1.0 + t) + (0.5 * root) * v * (1.0 - t * t) * (1.0 + 0.134145 * (v * v))
    pre_grad = (cot[...].astype(F32) * slope).astype(BF16)
    ngs[c] = (mm(pre_grad, wn[...], ((1,), (1,))) / divisor).astype(BF16)

    def ng_copy(k):
        return remote(ngs.at[c], ngs.at[c], ng_sems, k, col_to(k))

    each(1, C, lambda k: ng_copy(k).start())
    act_out[...] = (0.5 * v * (1.0 + t)).astype(BF16)
    agg_ref[...] = aggregate
    pre_ref[...] = pre_grad
    if m:
        for half, operand in enumerate((feat, agg_ref)):
            grads = mm(operand[...], pre_ref[...], ((0,), (0,))) * inv_root
            for local in range(D // m):
                d = half * (D // m) + local
                rd, cd, pd = d // (2 * C), d // 2 % C, d % 2
                piece = grads[local * m : (local + 1) * m].astype(BF16)
                gw_send[pd, cd, rd * m : (rd + 1) * m] = piece
        gw_copy = remote(gw_send.at[q], gw_sib, sib_sems, 1, sib)
        gw_copy.start()
    else:
        gw_out[:D] = mm(feat[...], pre_ref[...], ((0,), (0,))) * inv_root
        gw_out[D:] = mm(agg_ref[...], pre_ref[...], ((0,), (0,))) * inv_root
    sp_own[...] = mm(pre_ref[...], ws[...], ((1,), (1,)))

    each(1, C, lambda k: ng_copy(k).wait_recv())
    slab = ngs[...].reshape(C * T, D)

    def spread_to(row, rep):
        block = row * 2 + rep
        columns = asib[:, pl.ds(pl.multiple_of(block * T, T), T)]
        return mm(columns, slab, ((0,), (0,)))

    def sps_copy(k):
        return remote(sp_sib_send.at[k], sp_sib_recv.at[k], sps_sems, k, sib)

    def send_sib(k):
        sp_sib_send[k] = spread_to(lax.rem(r + k, R), q).astype(BF16)
        sps_copy(k).start()

    each(1, R, send_sib)
    send_sib(0)

    def sp_copy(k):
        return remote(sp_sib_recv.at[k], sp_recv.at[k], sp_sems, k, row_to(k))

    def send_spread(k):
        part = spread_to(lax.rem(r + k, R), p)
        sps_copy(k).wait_recv()
        sp_sib_recv[k] = (part + sp_sib_recv[k].astype(F32)).astype(BF16)
        sp_copy(k).start()

    each(1, R, send_spread)

    def gw1_copy(k):
        return remote(gw1_send.at[k], gw1_recv.at[k], gw1_sems, k, col_to(k))

    def gw2_copy(k):
        return remote(gw2_send.at[k], gw2_recv.at[k], gw2_sems, k, row_to(k))

    if m:
        gw_copy.wait()

        def gw_part(block):
            return gw_send[p, block].astype(F32) + gw_sib[block].astype(F32)

        for k in range(1, C):
            gw1_send[k] = gw_part(lax.rem(c + k, C)).astype(BF16)
            gw1_copy(k).start()
    part = spread_to(r, p)
    sps_copy(0).wait_recv()
    sp_own[...] += part + sp_sib_recv[0].astype(F32)
    if m:
        weights = gw_part(c)
        for k in range(1, C):
            gw1_copy(k).wait_recv()
            weights = weights + gw1_recv[k].astype(F32)
        gw_tot[...] = weights

        def gw_rows(row):
            return gw_tot[pl.ds(pl.multiple_of(row * m, m), m), :]

        for k in range(1, R):
            gw2_send[k] = gw_rows(lax.rem(r + k, R)).astype(BF16)
            gw2_copy(k).start()

    def add_spread(k):
        sp_copy(k).wait_recv()
        sp_own[...] += sp_recv[k].astype(F32)

    each(1, R, add_spread)
    gf_out[...] = sp_own[...].astype(BF16)
    if m:
        weights = gw_rows(r)
        for k in range(1, R):
            gw2_copy(k).wait_recv()
            weights = weights + gw2_recv[k].astype(F32)
        gw_out[...] = weights
        each(1, C, lambda k: gw1_copy(k).wait_send())
        each(1, R, lambda k: gw2_copy(k).wait_send())
    each(1, R, lambda k: feat_copy(k).wait_send())
    each(1, R, lambda k: fwd_copy(k).wait_send())
    fwd_copy(0).wait_send()
    each(1, C, lambda k: deg_copy(k).wait_send())
    each(1, C, lambda k: sum_copy(k).wait_send())
    each(1, C, lambda k: ng_copy(k).wait_send())
    each(0, R, lambda k: sps_copy(k).wait_send())
    each(1, R, lambda k: sp_copy(k).wait_send())


def shards(features, w_self, w_neigh, cotangent, tile_row, tile_col, tile_mask, tile_count):
    R, C = lax.axis_size("row"), lax.axis_size("col")
    ndev = R * C * 2
    T, D = features.shape
    m = 2 * D // ndev
    fused = m % 16 == 0
    m = m if fused else 0
    inv_root = 1.0 / math.sqrt(T * ndev)
    adjacency = build_adjacency(tile_row, tile_col, tile_count, tile_mask, C * 2, R * 2)
    adjacency = adjacency.reshape(2, C * T, R * 2 * T)
    V = pltpu.VMEM
    rows = max(m, 16)
    wr = rows * R if fused else 16
    dma = lambda n: pltpu.SemaphoreType.DMA((2, n))
    activated, grad_features, grads = pl.pallas_call(
        functools.partial(layer_kernel, R, C, m, inv_root),
        out_shape=(
            jax.ShapeDtypeStruct((T, D), BF16),
            jax.ShapeDtypeStruct((T, D), BF16),
            jax.ShapeDtypeStruct((m if fused else 2 * D, D), F32),
        ),
        in_specs=[pl.BlockSpec(memory_space=V)] * 5,
        out_specs=(pl.BlockSpec(memory_space=V),) * 3,
        scratch_shapes=[
            V((C * T, R * 2 * T), BF16),
            V((R * 2, T, D), BF16),
            V((C, 8, T), F32),
            V((C, 8, T), F32),
            V((C, T, D), BF16),
            V((C, T, D), BF16),
            V((T, D), F32),
            V((T, D), F32),
            V((T, D), BF16),
            V((T, D), BF16),
            V((C, T, D), BF16),
            V((R, T, D), BF16),
            V((R, T, D), BF16),
            V((R, T, D), BF16),
            V((T, D), F32),
            V((2, C, wr, D), BF16),
            V((C, wr, D), BF16),
            V((C, wr, D), BF16),
            V((C, wr, D), BF16),
            V((wr, D), F32),
            V((R, rows, D), BF16),
            V((R, rows, D), BF16),
            dma(2), dma(R), dma(R), dma(C), dma(C), dma(C), dma(R), dma(R), dma(C), dma(R),
        ],
        compiler_params=pltpu.CompilerParams(
            collective_id=0, has_side_effects=True, vmem_limit_bytes=60 * 2**20
        ),
    )(adjacency, features, w_self, w_neigh, cotangent)
    if not fused:
        grads = lax.psum_scatter(grads, ("row", "col", "rep"), scatter_dimension=0, tiled=True)
    return (activated, grad_features, grads)


def solution(mesh):
    placed = (
        P(("row", "col", "rep"), None),
        P(),
        P(),
        P(("row", "col", "rep"), None),
        P(("row", "col", "rep")),
        P(("row", "col", "rep")),
        P(("row", "col", "rep"), None, None),
        P(("row", "col", "rep")),
    )
    return jax.shard_map(
        shards,
        mesh=mesh,
        in_specs=placed,
        out_specs=(
            P(("row", "col", "rep"), None),
            P(("row", "col", "rep"), None),
            P(("row", "col", "rep"), None),
        ),
        check_vma=False,
    )
```

```python
import functools
import math

import jax
import jax.numpy as jnp
from jax import lax
from jax.experimental import pallas as pl
from jax.experimental.pallas import tpu as pltpu
from jax.sharding import PartitionSpec as P


def build_kernel(group, tile, row_blocks, rows_ref, cols_ref, count_ref, mask_ref, adj_ref):
    step = pl.program_id(0)

    @pl.when(step == 0)
    def _():
        adj_ref[...] = jnp.zeros_like(adj_ref)

    for lane in range(group):
        slot = step * group + lane

        @pl.when(slot < count_ref[0])
        def _():
            dest = rows_ref[slot]
            place = dest % 2 * (row_blocks // 2) + dest // 2
            row = pl.multiple_of(place * tile, tile)
            col = pl.multiple_of(cols_ref[slot] * tile, tile)
            where = (pl.ds(row, tile), pl.ds(col, tile))
            adj_ref[where] += mask_ref[lane].astype(jnp.float32).astype(jnp.bfloat16)


def build_adjacency(tile_row, tile_col, tile_count, tile_mask, row_blocks, col_blocks):
    slots, tile, _ = tile_mask.shape
    group = math.gcd(slots, 8)
    shape = (row_blocks * tile, col_blocks * tile)
    return pl.pallas_call(
        lambda *refs: build_kernel(group, tile, row_blocks, *refs),
        out_shape=jax.ShapeDtypeStruct(shape, jnp.bfloat16),
        grid_spec=pltpu.PrefetchScalarGridSpec(
            num_scalar_prefetch=3,
            grid=(slots // group,),
            in_specs=[pl.BlockSpec((group, tile, tile), lambda step, *_: (step, 0, 0))],
            out_specs=pl.BlockSpec(shape, lambda step, *_: (0, 0)),
        ),
        compiler_params=pltpu.CompilerParams(vmem_limit_bytes=48 * 2**20),
        cost_estimate=pl.CostEstimate(
            flops=slots * tile * tile, bytes_accessed=slots * tile * tile * 4, transcendentals=0
        ),
    )(tile_row, tile_col, tile_count, tile_mask)


MESH = pl.DeviceIdType.MESH
F32 = jnp.float32
BF16 = jnp.bfloat16


def each(start, stop, body):
    if stop - start <= 8:
        for k in range(start, stop):
            body(k)
    else:

        def step(k, carry):
            body(k)
            return carry

        lax.fori_loop(start, stop, step, 0)


def mm(a, b, dims=((1,), (0,))):
    return lax.dot_general(a, b, (dims, ((), ())), preferred_element_type=F32)


def layer_kernel(
    R, C, m, inv_root, inner, adj_hbm, row_ids, col_ids, count, feat, ws_hbm, wn_hbm, cot,
    act_out, gf_out, gw_out, *scratch
):
    (
        tiles, wide, adj, ws, wn, load_sems,
        asib, xg, deg_send, deg_recv, sum_send, sum_recv, own_sum, self_pre, agg_ref, pre_ref,
        ngs, sp_sib_send, sp_sib_recv, sp_recv, sp_own, gw_send, gw_sib, gw1_send,
        gw1_recv, gw_tot, gw2_send, gw2_recv, sib_sems, row_sems, fwd_sems, deg_sems, sum_sems,
        ng_sems, sps_sems, sp_sems, gw1_sems, gw2_sems,
    ) = scratch
    T, D = feat.shape
    r, c, p = lax.axis_index("row"), lax.axis_index("col"), lax.axis_index("rep")
    q = 1 - p
    ws_load = pltpu.make_async_copy(ws_hbm, ws, load_sems.at[0])
    wn_load = pltpu.make_async_copy(wn_hbm, wn, load_sems.at[1])
    adj_load = pltpu.make_async_copy(adj_hbm, tiles if inner else adj, load_sems.at[2])
    adj_load.start()
    ws_load.start()
    wn_load.start()
    barrier = pltpu.get_barrier_semaphore()
    pl.semaphore_signal(barrier, inc=1, device_id={"rep": q}, device_id_type=MESH)
    each(1, R, lambda k: pl.semaphore_signal(
        barrier, inc=1, device_id={"row": lax.rem(r + k, R)}, device_id_type=MESH))
    each(1, C, lambda k: pl.semaphore_signal(
        barrier, inc=1, device_id={"col": lax.rem(c + k, C)}, device_id_type=MESH))
    pl.semaphore_wait(barrier, R + C - 1)

    def remote(src, dst, sems, k, target):
        return pltpu.make_async_remote_copy(
            src_ref=src, dst_ref=dst, send_sem=sems.at[0, k], recv_sem=sems.at[1, k],
            device_id=target, device_id_type=MESH)

    def row_to(k):
        return {"row": lax.rem(r + k, R)}

    def col_to(k):
        return {"col": lax.rem(c + k, C)}

    sib = {"rep": q}
    mine = r * 2 + p

    def feat_copy(k):
        return remote(feat, xg.at[mine], row_sems, k, row_to(k))

    def fwd_copy(k):
        block = lax.rem(r + R - k, R) * 2 + p
        source = feat if isinstance(k, int) and k == 0 else xg.at[block]
        return remote(source, xg.at[block], fwd_sems, k, sib)

    each(1, R, lambda k: feat_copy(k).start())
    fwd_copy(0).start()
    adj_load.wait()
    if inner:
        slots = row_ids.shape[1]
        dest = row_ids[...]
        place = (dest & 1) * C + (dest >> 1)
        blocks = col_ids[...] * (2 * C) + place
        live = lax.broadcasted_iota(jnp.int32, (1, slots), 1) < count[...]
        blocks = jnp.where(live, blocks, -1)
        total_blocks = 4 * C * R
        pick = jnp.where(
            lax.broadcasted_iota(jnp.int32, (total_blocks, slots), 0) == blocks, 1.0, 0.0
        ).astype(BF16)

        def place_line(i, carry):
            line = tiles[pl.ds(i, slots, stride=T), :].astype(F32).astype(BF16)
            found = mm(pick, line)
            for j in range(2 * R):
                wide[j, pl.ds(i, 2 * C, stride=T), :] = found[j * 2 * C : (j + 1) * 2 * C]
            return carry

        lax.fori_loop(0, T, place_line, 0, unroll=4)
        for j in range(2 * R):
            for half in range(2):
                adj[half, :, j * T : (j + 1) * T] = wide[
                    j, half * C * T : (half + 1) * C * T, :
                ].astype(BF16)
    adj_copy = remote(adj.at[q], asib, sib_sems, 0, sib)
    adj_copy.start()
    xg[mine] = feat[...]
    ws_load.wait()
    wn_load.wait()
    self_pre[...] = mm(feat[...], ws[...])

    adj_copy.wait()
    asib[...] += adj[p]

    def rows_of(block):
        return asib[pl.ds(pl.multiple_of(block * T, T), T), :]

    ones = jnp.ones((8, asib.shape[1]), BF16)

    def deg_copy(k):
        return remote(deg_send.at[k], deg_recv.at[k], deg_sems, k, col_to(k))

    def send_degree(k):
        deg_send[k] = mm(ones, rows_of(lax.rem(c + k, C)), ((1,), (1,)))
        deg_copy(k).start()

    each(1, C, send_degree)
    degree = mm(ones, rows_of(c), ((1,), (1,)))

    def forward(k):
        feat_copy(k).wait_recv()
        fwd_copy(k).start()

    each(1, R, forward)
    each(0, R, lambda k: fwd_copy(k).wait_recv())
    sources = xg[...].reshape(R * 2 * T, D)

    def sum_copy(k):
        return remote(sum_send.at[k], sum_recv.at[k], sum_sems, k, col_to(k))

    def send_sum(k):
        sum_send[k] = mm(rows_of(lax.rem(c + k, C)), sources).astype(BF16)
        sum_copy(k).start()

    each(1, C, send_sum)
    own_sum[...] = mm(rows_of(c), sources)
    for k in range(1, C):
        deg_copy(k).wait_recv()
        degree = degree + deg_recv[k]
    diagonal = lax.broadcasted_iota(jnp.int32, (T, T), 0) == lax.broadcasted_iota(
        jnp.int32, (T, T), 1)
    spread_degree = jnp.broadcast_to(degree[0:1, :], (T, T))
    divisor = jnp.sum(jnp.where(diagonal, spread_degree, 0.0), axis=1, keepdims=True) + 1.0
    total = own_sum[...]
    for k in range(1, C):
        sum_copy(k).wait_recv()
        total = total + sum_recv[k].astype(F32)
    aggregate = (total / divisor).astype(BF16)
    v = self_pre[...] + mm(aggregate, wn[...])
    root = math.sqrt(2.0 / math.pi)
    t = jnp.tanh(root * (v + 0.044715 * (v * v * v)))
    slope = 0.5 * (1.0 + t) + (0.5 * root) * v * (1.0 - t * t) * (1.0 + 0.134145 * (v * v))
    pre_grad = (cot[...].astype(F32) * slope).astype(BF16)
    ngs[c] = (mm(pre_grad, wn[...], ((1,), (1,))) / divisor).astype(BF16)

    def ng_copy(k):
        return remote(ngs.at[c], ngs.at[c], ng_sems, k, col_to(k))

    each(1, C, lambda k: ng_copy(k).start())
    act_out[...] = (0.5 * v * (1.0 + t)).astype(BF16)
    agg_ref[...] = aggregate
    pre_ref[...] = pre_grad
    if m:
        for half, operand in enumerate((feat, agg_ref)):
            grads = mm(operand[...], pre_ref[...], ((0,), (0,))) * inv_root
            for local in range(D // m):
                d = half * (D // m) + local
                rd, cd, pd = d // (2 * C), d // 2 % C, d % 2
                piece = grads[local * m : (local + 1) * m].astype(BF16)
                gw_send[pd, cd, rd * m : (rd + 1) * m] = piece
        gw_copy = remote(gw_send.at[q], gw_sib, sib_sems, 1, sib)
        gw_copy.start()
    else:
        gw_out[:D] = mm(feat[...], pre_ref[...], ((0,), (0,))) * inv_root
        gw_out[D:] = mm(agg_ref[...], pre_ref[...], ((0,), (0,))) * inv_root
    sp_own[...] = mm(pre_ref[...], ws[...], ((1,), (1,)))

    each(1, C, lambda k: ng_copy(k).wait_recv())
    slab = ngs[...].reshape(C * T, D)

    def spread_to(row, rep):
        block = row * 2 + rep
        columns = asib[:, pl.ds(pl.multiple_of(block * T, T), T)]
        return mm(columns, slab, ((0,), (0,)))

    def sps_copy(k):
        return remote(sp_sib_send.at[k], sp_sib_recv.at[k], sps_sems, k, sib)

    def send_sib(k):
        sp_sib_send[k] = spread_to(lax.rem(r + k, R), q).astype(BF16)
        sps_copy(k).start()

    each(1, R, send_sib)
    send_sib(0)

    def sp_copy(k):
        return remote(sp_sib_recv.at[k], sp_recv.at[k], sp_sems, k, row_to(k))

    def send_spread(k):
        part = spread_to(lax.rem(r + k, R), p)
        sps_copy(k).wait_recv()
        sp_sib_recv[k] = (part + sp_sib_recv[k].astype(F32)).astype(BF16)
        sp_copy(k).start()

    each(1, R, send_spread)

    def gw1_copy(k):
        return remote(gw1_send.at[k], gw1_recv.at[k], gw1_sems, k, col_to(k))

    def gw2_copy(k):
        return remote(gw2_send.at[k], gw2_recv.at[k], gw2_sems, k, row_to(k))

    if m:
        gw_copy.wait()

        def gw_part(block):
            return gw_send[p, block].astype(F32) + gw_sib[block].astype(F32)

        for k in range(1, C):
            gw1_send[k] = gw_part(lax.rem(c + k, C)).astype(BF16)
            gw1_copy(k).start()
    part = spread_to(r, p)
    sps_copy(0).wait_recv()
    sp_own[...] += part + sp_sib_recv[0].astype(F32)
    if m:
        weights = gw_part(c)
        for k in range(1, C):
            gw1_copy(k).wait_recv()
            weights = weights + gw1_recv[k].astype(F32)
        gw_tot[...] = weights

        def gw_rows(row):
            return gw_tot[pl.ds(pl.multiple_of(row * m, m), m), :]

        for k in range(1, R):
            gw2_send[k] = gw_rows(lax.rem(r + k, R)).astype(BF16)
            gw2_copy(k).start()

    def add_spread(k):
        sp_copy(k).wait_recv()
        sp_own[...] += sp_recv[k].astype(F32)

    each(1, R, add_spread)
    gf_out[...] = sp_own[...].astype(BF16)
    if m:
        weights = gw_rows(r)
        for k in range(1, R):
            gw2_copy(k).wait_recv()
            weights = weights + gw2_recv[k].astype(F32)
        gw_out[...] = weights
        each(1, C, lambda k: gw1_copy(k).wait_send())
        each(1, R, lambda k: gw2_copy(k).wait_send())
    each(1, R, lambda k: feat_copy(k).wait_send())
    each(1, R, lambda k: fwd_copy(k).wait_send())
    fwd_copy(0).wait_send()
    each(1, C, lambda k: deg_copy(k).wait_send())
    each(1, C, lambda k: sum_copy(k).wait_send())
    each(1, C, lambda k: ng_copy(k).wait_send())
    each(0, R, lambda k: sps_copy(k).wait_send())
    each(1, R, lambda k: sp_copy(k).wait_send())


def copy_kernel(a, b, c, to_a, to_b, to_c, sems):
    pairs = ((a, to_a), (b, to_b), (c, to_c))
    copies = [pltpu.make_async_copy(x, y, sems.at[k]) for k, (x, y) in enumerate(pairs)]
    for copy in copies:
        copy.start()
    for copy in copies:
        copy.wait()


def shards(features, w_self, w_neigh, cotangent, tile_row, tile_col, tile_mask, tile_count):
    R, C = lax.axis_size("row"), lax.axis_size("col")
    ndev = R * C * 2
    T, D = features.shape
    m = 2 * D // ndev
    fused = m % 16 == 0
    m = m if fused else 0
    inv_root = 1.0 / math.sqrt(T * ndev)
    slots = tile_row.shape[0]
    inner = R * C <= 16
    if inner:
        adjacency = tile_mask.reshape(slots * T, T)
    else:
        adjacency = build_adjacency(tile_row, tile_col, tile_count, tile_mask, C * 2, R * 2)
        adjacency = adjacency.reshape(2, C * T, R * 2 * T)
    V = pltpu.VMEM
    rows = max(m, 16)
    wr = rows * R if fused else 16
    dma = lambda n: pltpu.SemaphoreType.DMA((2, n))
    vm, hbm = pl.BlockSpec(memory_space=V), pl.BlockSpec(memory_space=pl.ANY)
    results = pl.pallas_call(
        functools.partial(layer_kernel, R, C, m, inv_root, inner),
        out_shape=(
            jax.ShapeDtypeStruct((T, D), BF16),
            jax.ShapeDtypeStruct((T, D), BF16),
            jax.ShapeDtypeStruct((m if fused else 2 * D, D), F32),
        ),
        in_specs=[hbm, vm, vm, vm, vm, hbm, hbm, vm],
        out_specs=(pl.BlockSpec(memory_space=V),) * 3,
        scratch_shapes=[
            V((slots * T, T) if inner else (8, T), jnp.int32),
            V((2 * R, 2 * C * T, T) if inner else (1, 8, T), F32),
            V((2, C * T, R * 2 * T), BF16),
            V((D, D), BF16),
            V((D, D), BF16),
            pltpu.SemaphoreType.DMA((3,)),
            V((C * T, R * 2 * T), BF16),
            V((R * 2, T, D), BF16),
            V((C, 8, T), F32),
            V((C, 8, T), F32),
            V((C, T, D), BF16),
            V((C, T, D), BF16),
            V((T, D), F32),
            V((T, D), F32),
            V((T, D), BF16),
            V((T, D), BF16),
            V((C, T, D), BF16),
            V((R, T, D), BF16),
            V((R, T, D), BF16),
            V((R, T, D), BF16),
            V((T, D), F32),
            V((2, C, wr, D), BF16),
            V((C, wr, D), BF16),
            V((C, wr, D), BF16),
            V((C, wr, D), BF16),
            V((wr, D), F32),
            V((R, rows, D), BF16),
            V((R, rows, D), BF16),
            dma(2), dma(R), dma(R), dma(C), dma(C), dma(C), dma(R), dma(R), dma(C), dma(R),
        ],
        compiler_params=pltpu.CompilerParams(
            collective_id=0, has_side_effects=True, vmem_limit_bytes=60 * 2**20
        ),
    )(
        adjacency,
        tile_row.reshape(1, slots),
        tile_col.reshape(1, slots),
        tile_count.reshape(1, 1),
        features,
        w_self,
        w_neigh,
        cotangent,
    )
    activated, grad_features, grads = pl.pallas_call(
        copy_kernel,
        out_shape=tuple(jax.ShapeDtypeStruct(x.shape, x.dtype) for x in results),
        in_specs=[hbm] * 3,
        out_specs=(hbm,) * 3,
        scratch_shapes=[pltpu.SemaphoreType.DMA((3,))],
    )(*results)
    if not fused:
        grads = lax.psum_scatter(grads, ("row", "col", "rep"), scatter_dimension=0, tiled=True)
    return (activated, grad_features, grads)


def solution(mesh):
    placed = (
        P(("row", "col", "rep"), None),
        P(),
        P(),
        P(("row", "col", "rep"), None),
        P(("row", "col", "rep")),
        P(("row", "col", "rep")),
        P(("row", "col", "rep"), None, None),
        P(("row", "col", "rep")),
    )
    return jax.shard_map(
        shards,
        mesh=mesh,
        in_specs=placed,
        out_specs=(
            P(("row", "col", "rep"), None),
            P(("row", "col", "rep"), None),
            P(("row", "col", "rep"), None),
        ),
        check_vma=False,
    )
```

```python
import functools
import math

import jax
import jax.numpy as jnp
from jax import lax
from jax.experimental import pallas as pl
from jax.experimental.pallas import tpu as pltpu
from jax.sharding import PartitionSpec as P


def build_kernel(group, tile, row_blocks, rows_ref, cols_ref, count_ref, mask_ref, adj_ref):
    step = pl.program_id(0)

    @pl.when(step == 0)
    def _():
        adj_ref[...] = jnp.zeros_like(adj_ref)

    for lane in range(group):
        slot = step * group + lane

        @pl.when(slot < count_ref[0])
        def _():
            dest = rows_ref[slot]
            place = dest % 2 * (row_blocks // 2) + dest // 2
            row = pl.multiple_of(place * tile, tile)
            col = pl.multiple_of(cols_ref[slot] * tile, tile)
            where = (pl.ds(row, tile), pl.ds(col, tile))
            adj_ref[where] += mask_ref[lane].astype(jnp.float32).astype(jnp.bfloat16)


def build_adjacency(tile_row, tile_col, tile_count, tile_mask, row_blocks, col_blocks):
    slots, tile, _ = tile_mask.shape
    group = math.gcd(slots, 8)
    shape = (row_blocks * tile, col_blocks * tile)
    return pl.pallas_call(
        lambda *refs: build_kernel(group, tile, row_blocks, *refs),
        out_shape=jax.ShapeDtypeStruct(shape, jnp.bfloat16),
        grid_spec=pltpu.PrefetchScalarGridSpec(
            num_scalar_prefetch=3,
            grid=(slots // group,),
            in_specs=[pl.BlockSpec((group, tile, tile), lambda step, *_: (step, 0, 0))],
            out_specs=pl.BlockSpec(shape, lambda step, *_: (0, 0)),
        ),
        compiler_params=pltpu.CompilerParams(vmem_limit_bytes=48 * 2**20),
        cost_estimate=pl.CostEstimate(
            flops=slots * tile * tile, bytes_accessed=slots * tile * tile * 4, transcendentals=0
        ),
    )(tile_row, tile_col, tile_count, tile_mask)


MESH = pl.DeviceIdType.MESH
F32 = jnp.float32
BF16 = jnp.bfloat16
H = 2


def each(start, stop, body):
    if stop - start <= 8:
        for k in range(start, stop):
            body(k)
    else:

        def step(k, carry):
            body(k)
            return carry

        lax.fori_loop(start, stop, step, 0)


def mm(a, b, dims=((1,), (0,))):
    return lax.dot_general(a, b, (dims, ((), ())), preferred_element_type=F32)


def layer_kernel(
    R, C, m, inv_root, inner, adj_hbm, row_ids, col_ids, count, feat, ws_hbm, wn_hbm, cot,
    act_out, gf_out, gw_out, *scratch
):
    (
        tiles, wide, adj, turned, ws, wn, load_sems,
        asib, xg, deg_send, deg_recv, sum_send, sum_recv, own_sum, self_pre, agg_ref, pre_ref,
        ngs, sp_sib_send, sp_sib_recv, sp_recv, sp_own, gw_send, gw_sib, gw1_send,
        gw1_recv, gw_tot, gw2_send, gw2_recv, sib_sems, row_sems, fwd_sems, deg_sems, sum_sems,
        ng_sems, sps_sems, sp_sems, gw1_sems, gw2_sems,
    ) = scratch
    T, D = feat.shape
    W = D // H
    parts = [slice(h * W, (h + 1) * W) for h in range(H)]
    r, c, p = lax.axis_index("row"), lax.axis_index("col"), lax.axis_index("rep")
    q = 1 - p
    ws_load = pltpu.make_async_copy(ws_hbm, ws, load_sems.at[0])
    wn_load = pltpu.make_async_copy(wn_hbm, wn, load_sems.at[1])
    adj_load = pltpu.make_async_copy(adj_hbm, tiles if inner else adj, load_sems.at[2])
    adj_load.start()
    ws_load.start()
    wn_load.start()
    barrier = pltpu.get_barrier_semaphore()
    pl.semaphore_signal(barrier, inc=1, device_id={"rep": q}, device_id_type=MESH)
    each(1, R, lambda k: pl.semaphore_signal(
        barrier, inc=1, device_id={"row": lax.rem(r + k, R)}, device_id_type=MESH))
    each(1, C, lambda k: pl.semaphore_signal(
        barrier, inc=1, device_id={"col": lax.rem(c + k, C)}, device_id_type=MESH))
    pl.semaphore_wait(barrier, R + C - 1)

    def remote(src, dst, sems, k, target):
        return pltpu.make_async_remote_copy(
            src_ref=src, dst_ref=dst, send_sem=sems.at[0, k], recv_sem=sems.at[1, k],
            device_id=target, device_id_type=MESH)

    def row_to(k):
        return {"row": lax.rem(r + k, R)}

    def col_to(k):
        return {"col": lax.rem(c + k, C)}

    sib = {"rep": q}
    mine = r * 2 + p

    def feat_copy(k, h):
        source = feat.at[:, parts[h]]
        return remote(source, xg.at[h, mine], row_sems, k * H + h, row_to(k))

    def fwd_copy(k, h):
        block = lax.rem(r + R - k, R) * 2 + p
        own = isinstance(k, int) and k == 0
        source = feat.at[:, parts[h]] if own else xg.at[h, block]
        return remote(source, xg.at[h, block], fwd_sems, k * H + h, sib)

    for h in range(H):
        each(1, R, lambda k: feat_copy(k, h).start())
    for h in range(H):
        fwd_copy(0, h).start()
    adj_load.wait()
    if inner:
        slots = row_ids.shape[1]
        dest = row_ids[...]
        place = (dest & 1) * C + (dest >> 1)
        blocks = col_ids[...] * (2 * C) + place
        live = lax.broadcasted_iota(jnp.int32, (1, slots), 1) < count[...]
        blocks = jnp.where(live, blocks, -1)
        total_blocks = 4 * C * R
        pick = jnp.where(
            lax.broadcasted_iota(jnp.int32, (total_blocks, slots), 0) == blocks, 1.0, 0.0
        ).astype(BF16)

        def place_line(i, carry):
            line = tiles[pl.ds(i, slots, stride=T), :].astype(F32).astype(BF16)
            found = mm(pick, line)
            for j in range(2 * R):
                wide[j, pl.ds(i, 2 * C, stride=T), :] = found[j * 2 * C : (j + 1) * 2 * C]
            return carry

        lax.fori_loop(0, T, place_line, 0, unroll=4)
        for j in range(2 * R):
            for half in range(2):
                adj[half, :, j * T : (j + 1) * T] = wide[
                    j, half * C * T : (half + 1) * C * T, :
                ].astype(BF16)
    adj_copy = remote(adj.at[q], asib, sib_sems, 0, sib)
    adj_copy.start()
    for h in range(H):
        xg[h, mine] = feat[:, parts[h]]
    ws_load.wait()
    wn_load.wait()
    self_pre[...] = mm(feat[...], ws[...])

    adj_copy.wait()
    asib[...] += adj[p]

    def rows_of(block):
        return asib[pl.ds(pl.multiple_of(block * T, T), T), :]

    ones = jnp.ones((8, asib.shape[1]), BF16)

    def deg_copy(k):
        return remote(deg_send.at[k], deg_recv.at[k], deg_sems, k, col_to(k))

    def send_degree(k):
        deg_send[k] = mm(ones, rows_of(lax.rem(c + k, C)), ((1,), (1,)))
        deg_copy(k).start()

    each(1, C, send_degree)
    degree = mm(ones, rows_of(c), ((1,), (1,)))

    if inner:
        turned[...] = asib[...].T

    def sum_copy(k, h):
        return remote(sum_send.at[h, k], sum_recv.at[h, k], sum_sems, k * H + h, col_to(k))

    def forward(k, h):
        feat_copy(k, h).wait_recv()
        fwd_copy(k, h).start()

    for h in range(H):
        each(1, R, lambda k: forward(k, h))
        each(0, R, lambda k: fwd_copy(k, h).wait_recv())
        sources = xg[h].reshape(R * 2 * T, W)

        def send_sum(k):
            sum_send[h, k] = mm(rows_of(lax.rem(c + k, C)), sources).astype(BF16)
            sum_copy(k, h).start()

        each(1, C, send_sum)
        own_sum[:, parts[h]] = mm(rows_of(c), sources)
    for k in range(1, C):
        deg_copy(k).wait_recv()
        degree = degree + deg_recv[k]
    diagonal = lax.broadcasted_iota(jnp.int32, (T, T), 0) == lax.broadcasted_iota(
        jnp.int32, (T, T), 1)
    spread_degree = jnp.broadcast_to(degree[0:1, :], (T, T))
    divisor = jnp.sum(jnp.where(diagonal, spread_degree, 0.0), axis=1, keepdims=True) + 1.0
    for h in range(H):
        for k in range(1, C):
            sum_copy(k, h).wait_recv()
            own_sum[:, parts[h]] += sum_recv[h, k].astype(F32)
    total = own_sum[...]
    aggregate = (total / divisor).astype(BF16)
    v = self_pre[...] + mm(aggregate, wn[...])
    root = math.sqrt(2.0 / math.pi)
    t = jnp.tanh(root * (v + 0.044715 * (v * v * v)))
    slope = 0.5 * (1.0 + t) + (0.5 * root) * v * (1.0 - t * t) * (1.0 + 0.134145 * (v * v))
    pre_grad = (cot[...].astype(F32) * slope).astype(BF16)

    def ng_copy(k, h):
        return remote(ngs.at[h, c], ngs.at[h, c], ng_sems, k * H + h, col_to(k))

    for h in range(H):
        ngs[h, c] = (mm(pre_grad, wn[parts[h], :], ((1,), (1,))) / divisor).astype(BF16)
        each(1, C, lambda k: ng_copy(k, h).start())
    act_out[...] = (0.5 * v * (1.0 + t)).astype(BF16)
    agg_ref[...] = aggregate
    pre_ref[...] = pre_grad
    if m:
        for half, operand in enumerate((feat, agg_ref)):
            grads = mm(operand[...], pre_ref[...], ((0,), (0,))) * inv_root
            for local in range(D // m):
                d = half * (D // m) + local
                rd, cd, pd = d // (2 * C), d // 2 % C, d % 2
                piece = grads[local * m : (local + 1) * m].astype(BF16)
                gw_send[pd, cd, rd * m : (rd + 1) * m] = piece
        gw_copy = remote(gw_send.at[q], gw_sib, sib_sems, 1, sib)
        gw_copy.start()
    else:
        gw_out[:D] = mm(feat[...], pre_ref[...], ((0,), (0,))) * inv_root
        gw_out[D:] = mm(agg_ref[...], pre_ref[...], ((0,), (0,))) * inv_root
    sp_own[...] = mm(pre_ref[...], ws[...], ((1,), (1,)))

    def spread_to(row, rep, h):
        block = row * 2 + rep
        slab = ngs[h].reshape(C * T, W)
        lines = pl.ds(pl.multiple_of(block * T, T), T)
        if inner:
            return mm(turned[lines, :], slab)
        return mm(asib[:, lines], slab, ((0,), (0,)))

    def sps_copy(k, h):
        return remote(sp_sib_send.at[h, k], sp_sib_recv.at[h, k], sps_sems, k * H + h, sib)

    def sp_copy(k, h):
        return remote(sp_sib_recv.at[h, k], sp_recv.at[h, k], sp_sems, k * H + h, row_to(k))

    for h in range(H):
        each(1, C, lambda k: ng_copy(k, h).wait_recv())

        def send_sib(k):
            sp_sib_send[h, k] = spread_to(lax.rem(r + k, R), q, h).astype(BF16)
            sps_copy(k, h).start()

        each(1, R, send_sib)
        send_sib(0)

        def send_spread(k):
            part = spread_to(lax.rem(r + k, R), p, h)
            sps_copy(k, h).wait_recv()
            sp_sib_recv[h, k] = (part + sp_sib_recv[h, k].astype(F32)).astype(BF16)
            sp_copy(k, h).start()

        each(1, R, send_spread)

    def gw1_copy(k):
        return remote(gw1_send.at[k], gw1_recv.at[k], gw1_sems, k, col_to(k))

    def gw2_copy(k):
        return remote(gw2_send.at[k], gw2_recv.at[k], gw2_sems, k, row_to(k))

    if m:
        gw_copy.wait()

        def gw_part(block):
            return gw_send[p, block].astype(F32) + gw_sib[block].astype(F32)

        for k in range(1, C):
            gw1_send[k] = gw_part(lax.rem(c + k, C)).astype(BF16)
            gw1_copy(k).start()
    for h in range(H):
        part = spread_to(r, p, h)
        sps_copy(0, h).wait_recv()
        sp_own[:, parts[h]] += part + sp_sib_recv[h, 0].astype(F32)
    if m:
        weights = gw_part(c)
        for k in range(1, C):
            gw1_copy(k).wait_recv()
            weights = weights + gw1_recv[k].astype(F32)
        gw_tot[...] = weights

        def gw_rows(row):
            return gw_tot[pl.ds(pl.multiple_of(row * m, m), m), :]

        for k in range(1, R):
            gw2_send[k] = gw_rows(lax.rem(r + k, R)).astype(BF16)
            gw2_copy(k).start()

    for h in range(H):

        def add_spread(k):
            sp_copy(k, h).wait_recv()
            sp_own[:, parts[h]] += sp_recv[h, k].astype(F32)

        each(1, R, add_spread)
    gf_out[...] = sp_own[...].astype(BF16)
    if m:
        weights = gw_rows(r)
        for k in range(1, R):
            gw2_copy(k).wait_recv()
            weights = weights + gw2_recv[k].astype(F32)
        gw_out[...] = weights
        each(1, C, lambda k: gw1_copy(k).wait_send())
        each(1, R, lambda k: gw2_copy(k).wait_send())
    each(1, C, lambda k: deg_copy(k).wait_send())
    for h in range(H):
        each(1, R, lambda k: feat_copy(k, h).wait_send())
        each(1, R, lambda k: fwd_copy(k, h).wait_send())
        fwd_copy(0, h).wait_send()
        each(1, C, lambda k: sum_copy(k, h).wait_send())
        each(1, C, lambda k: ng_copy(k, h).wait_send())
        each(0, R, lambda k: sps_copy(k, h).wait_send())
        each(1, R, lambda k: sp_copy(k, h).wait_send())


def copy_kernel(a, b, c, to_a, to_b, to_c):
    to_a[...] = a[...]
    to_b[...] = b[...]
    to_c[...] = c[...]


def shards(features, w_self, w_neigh, cotangent, tile_row, tile_col, tile_mask, tile_count):
    R, C = lax.axis_size("row"), lax.axis_size("col")
    ndev = R * C * 2
    T, D = features.shape
    m = 2 * D // ndev
    fused = m % 16 == 0
    m = m if fused else 0
    inv_root = 1.0 / math.sqrt(T * ndev)
    slots = tile_row.shape[0]
    inner = R * C <= 16
    if inner:
        adjacency = tile_mask.reshape(slots * T, T)
    else:
        adjacency = build_adjacency(tile_row, tile_col, tile_count, tile_mask, C * 2, R * 2)
        adjacency = adjacency.reshape(2, C * T, R * 2 * T)
    V = pltpu.VMEM
    rows = max(m, 16)
    wr = rows * R if fused else 16
    dma = lambda n: pltpu.SemaphoreType.DMA((2, n))
    vm, hbm = pl.BlockSpec(memory_space=V), pl.BlockSpec(memory_space=pl.ANY)
    results = pl.pallas_call(
        functools.partial(layer_kernel, R, C, m, inv_root, inner),
        out_shape=(
            jax.ShapeDtypeStruct((T, D), BF16),
            jax.ShapeDtypeStruct((T, D), BF16),
            jax.ShapeDtypeStruct((m if fused else 2 * D, D), F32),
        ),
        in_specs=[hbm, vm, vm, vm, vm, hbm, hbm, vm],
        out_specs=(pl.BlockSpec(memory_space=V),) * 3,
        scratch_shapes=[
            V((slots * T, T) if inner else (8, T), jnp.int32),
            V((2 * R, 2 * C * T, T) if inner else (1, 8, T), F32),
            V((2, C * T, R * 2 * T), BF16),
            V((R * 2 * T, C * T) if inner else (16, T), BF16),
            V((D, D), BF16),
            V((D, D), BF16),
            pltpu.SemaphoreType.DMA((3,)),
            V((C * T, R * 2 * T), BF16),
            V((H, R * 2, T, D // H), BF16),
            V((C, 8, T), F32),
            V((C, 8, T), F32),
            V((H, C, T, D // H), BF16),
            V((H, C, T, D // H), BF16),
            V((T, D), F32),
            V((T, D), F32),
            V((T, D), BF16),
            V((T, D), BF16),
            V((H, C, T, D // H), BF16),
            V((H, R, T, D // H), BF16),
            V((H, R, T, D // H), BF16),
            V((H, R, T, D // H), BF16),
            V((T, D), F32),
            V((2, C, wr, D), BF16),
            V((C, wr, D), BF16),
            V((C, wr, D), BF16),
            V((C, wr, D), BF16),
            V((wr, D), F32),
            V((R, rows, D), BF16),
            V((R, rows, D), BF16),
            dma(2), dma(R * H), dma(R * H), dma(C), dma(C * H), dma(C * H), dma(R * H), dma(R * H),
            dma(C), dma(R),
        ],
        compiler_params=pltpu.CompilerParams(
            collective_id=0, has_side_effects=True, vmem_limit_bytes=60 * 2**20
        ),
    )(
        adjacency,
        tile_row.reshape(1, slots),
        tile_col.reshape(1, slots),
        tile_count.reshape(1, 1),
        features,
        w_self,
        w_neigh,
        cotangent,
    )
    activated, grad_features, grads = pl.pallas_call(
        copy_kernel,
        out_shape=tuple(jax.ShapeDtypeStruct(x.shape, x.dtype) for x in results),
        in_specs=[vm] * 3,
        out_specs=(vm,) * 3,
    )(*results)
    if not fused:
        grads = lax.psum_scatter(grads, ("row", "col", "rep"), scatter_dimension=0, tiled=True)
    return (activated, grad_features, grads)


def solution(mesh):
    placed = (
        P(("row", "col", "rep"), None),
        P(),
        P(),
        P(("row", "col", "rep"), None),
        P(("row", "col", "rep")),
        P(("row", "col", "rep")),
        P(("row", "col", "rep"), None, None),
        P(("row", "col", "rep")),
    )
    return jax.shard_map(
        shards,
        mesh=mesh,
        in_specs=placed,
        out_specs=(
            P(("row", "col", "rep"), None),
            P(("row", "col", "rep"), None),
            P(("row", "col", "rep"), None),
        ),
        check_vma=False,
    )
```

```python
import functools
import math

import jax
import jax.numpy as jnp
from jax import lax
from jax.experimental import pallas as pl
from jax.experimental.pallas import tpu as pltpu
from jax.sharding import PartitionSpec as P


def build_kernel(group, tile, row_blocks, rows_ref, cols_ref, count_ref, mask_ref, adj_ref):
    step = pl.program_id(0)

    @pl.when(step == 0)
    def _():
        adj_ref[...] = jnp.zeros_like(adj_ref)

    for lane in range(group):
        slot = step * group + lane

        @pl.when(slot < count_ref[0])
        def _():
            dest = rows_ref[slot]
            place = dest % 2 * (row_blocks // 2) + dest // 2
            row = pl.multiple_of(place * tile, tile)
            col = pl.multiple_of(cols_ref[slot] * tile, tile)
            where = (pl.ds(row, tile), pl.ds(col, tile))
            adj_ref[where] += mask_ref[lane].astype(jnp.float32).astype(jnp.bfloat16)


def build_adjacency(tile_row, tile_col, tile_count, tile_mask, row_blocks, col_blocks):
    slots, tile, _ = tile_mask.shape
    group = math.gcd(slots, 8)
    shape = (row_blocks * tile, col_blocks * tile)
    return pl.pallas_call(
        lambda *refs: build_kernel(group, tile, row_blocks, *refs),
        out_shape=jax.ShapeDtypeStruct(shape, jnp.bfloat16),
        grid_spec=pltpu.PrefetchScalarGridSpec(
            num_scalar_prefetch=3,
            grid=(slots // group,),
            in_specs=[pl.BlockSpec((group, tile, tile), lambda step, *_: (step, 0, 0))],
            out_specs=pl.BlockSpec(shape, lambda step, *_: (0, 0)),
        ),
        compiler_params=pltpu.CompilerParams(vmem_limit_bytes=48 * 2**20),
        cost_estimate=pl.CostEstimate(
            flops=slots * tile * tile, bytes_accessed=slots * tile * tile * 4, transcendentals=0
        ),
    )(tile_row, tile_col, tile_count, tile_mask)


MESH = pl.DeviceIdType.MESH
F32 = jnp.float32
BF16 = jnp.bfloat16
H = 2


def each(start, stop, body):
    if stop - start <= 8:
        for k in range(start, stop):
            body(k)
    else:

        def step(k, carry):
            body(k)
            return carry

        lax.fori_loop(start, stop, step, 0)


def mm(a, b, dims=((1,), (0,))):
    return lax.dot_general(a, b, (dims, ((), ())), preferred_element_type=F32)


def layer_kernel(
    R, C, m, inv_root, inner, adj_hbm, row_ids, col_ids, count, feat, ws_hbm, wn_hbm, cot,
    act_out, gf_out, gw_out, *scratch
):
    (
        tiles, wide, adj, turned, ws, wn, load_sems,
        asib, xg, deg_send, deg_recv, sum_send, sum_recv, own_sum, self_pre, agg_ref, pre_ref,
        ngs, sp_sib_send, sp_sib_recv, sp_recv, sp_own, gw_send, gw_sib, gw1_send,
        gw1_recv, gw_tot, gw2_send, gw2_recv, sib_sems, row_sems, fwd_sems, deg_sems, sum_sems,
        ng_sems, sps_sems, sp_sems, gw1_sems, gw2_sems,
    ) = scratch
    T, D = feat.shape
    W = D // H
    parts = [slice(h * W, (h + 1) * W) for h in range(H)]
    r, c, p = lax.axis_index("row"), lax.axis_index("col"), lax.axis_index("rep")
    q = 1 - p
    ws_load = pltpu.make_async_copy(ws_hbm, ws, load_sems.at[0])
    wn_load = pltpu.make_async_copy(wn_hbm, wn, load_sems.at[1])
    adj_load = pltpu.make_async_copy(adj_hbm, tiles if inner else adj, load_sems.at[2])
    adj_load.start()
    ws_load.start()
    wn_load.start()
    barrier = pltpu.get_barrier_semaphore()
    pl.semaphore_signal(barrier, inc=1, device_id={"rep": q}, device_id_type=MESH)
    each(1, R, lambda k: pl.semaphore_signal(
        barrier, inc=1, device_id={"row": lax.rem(r + k, R)}, device_id_type=MESH))
    each(1, C, lambda k: pl.semaphore_signal(
        barrier, inc=1, device_id={"col": lax.rem(c + k, C)}, device_id_type=MESH))
    pl.semaphore_wait(barrier, R + C - 1)

    def remote(src, dst, sems, k, target):
        return pltpu.make_async_remote_copy(
            src_ref=src, dst_ref=dst, send_sem=sems.at[0, k], recv_sem=sems.at[1, k],
            device_id=target, device_id_type=MESH)

    def row_to(k):
        return {"row": lax.rem(r + k, R)}

    def col_to(k):
        return {"col": lax.rem(c + k, C)}

    sib = {"rep": q}
    mine = r * 2 + p

    def feat_copy(k, h):
        source = feat.at[:, parts[h]]
        return remote(source, xg.at[h, mine], row_sems, k * H + h, row_to(k))

    def fwd_copy(k, h):
        block = lax.rem(r + R - k, R) * 2 + p
        own = isinstance(k, int) and k == 0
        source = feat.at[:, parts[h]] if own else xg.at[h, block]
        return remote(source, xg.at[h, block], fwd_sems, k * H + h, sib)

    for h in range(H):
        each(1, R, lambda k: feat_copy(k, h).start())
    for h in range(H):
        fwd_copy(0, h).start()
    adj_load.wait()
    if inner:
        slots = row_ids.shape[1]
        dest = row_ids[...]
        place = (dest & 1) * C + (dest >> 1)
        blocks = col_ids[...] * (2 * C) + place
        live = lax.broadcasted_iota(jnp.int32, (1, slots), 1) < count[...]
        blocks = jnp.where(live, blocks, -1)
        total_blocks = 4 * C * R
        pick = jnp.where(
            lax.broadcasted_iota(jnp.int32, (total_blocks, slots), 0) == blocks, 1.0, 0.0
        ).astype(BF16)

        def place_line(i, carry):
            lines = [
                tiles[pl.ds(2 * i + e, slots, stride=T), :].astype(F32).astype(BF16)
                for e in range(2)
            ]
            found = mm(pick, jnp.concatenate(lines, axis=1))
            for e in range(2):
                for j in range(2 * R):
                    wide[j, pl.ds(2 * i + e, 2 * C, stride=T), :] = found[
                        j * 2 * C : (j + 1) * 2 * C, e * T : (e + 1) * T
                    ]
            return carry

        lax.fori_loop(0, T // 2, place_line, 0, unroll=4)
        for j in range(2 * R):
            for half in range(2):
                adj[half, :, j * T : (j + 1) * T] = wide[
                    j, half * C * T : (half + 1) * C * T, :
                ].astype(BF16)
    adj_copy = remote(adj.at[q], asib, sib_sems, 0, sib)
    adj_copy.start()
    for h in range(H):
        xg[h, mine] = feat[:, parts[h]]
    ws_load.wait()
    wn_load.wait()
    self_pre[...] = mm(feat[...], ws[...])

    def forward(k, h):
        feat_copy(k, h).wait_recv()
        fwd_copy(k, h).start()

    each(1, R, lambda k: forward(k, 0))
    adj_copy.wait()
    asib[...] += adj[p]

    def rows_of(block):
        return asib[pl.ds(pl.multiple_of(block * T, T), T), :]

    def sum_copy(k, h):
        return remote(sum_send.at[h, k], sum_recv.at[h, k], sum_sems, k * H + h, col_to(k))

    for h in range(H):
        if h > 0:
            each(1, R, lambda k: forward(k, h))
        each(0, R, lambda k: fwd_copy(k, h).wait_recv())
        sources = xg[h].reshape(R * 2 * T, W)

        def send_sum(k):
            sum_send[h, k] = mm(rows_of(lax.rem(c + k, C)), sources).astype(BF16)
            sum_copy(k, h).start()

        each(1, C, send_sum)
        own_sum[:, parts[h]] = mm(rows_of(c), sources)
    ones = jnp.ones((8, asib.shape[1]), BF16)

    def deg_copy(k):
        return remote(deg_send.at[k], deg_recv.at[k], deg_sems, k, col_to(k))

    def send_degree(k):
        deg_send[k] = mm(ones, rows_of(lax.rem(c + k, C)), ((1,), (1,)))
        deg_copy(k).start()

    each(1, C, send_degree)
    degree = mm(ones, rows_of(c), ((1,), (1,)))

    if inner:
        turned[...] = asib[...].T

    for k in range(1, C):
        deg_copy(k).wait_recv()
        degree = degree + deg_recv[k]
    diagonal = lax.broadcasted_iota(jnp.int32, (T, T), 0) == lax.broadcasted_iota(
        jnp.int32, (T, T), 1)
    spread_degree = jnp.broadcast_to(degree[0:1, :], (T, T))
    divisor = jnp.sum(jnp.where(diagonal, spread_degree, 0.0), axis=1, keepdims=True) + 1.0
    for h in range(H):
        for k in range(1, C):
            sum_copy(k, h).wait_recv()
            own_sum[:, parts[h]] += sum_recv[h, k].astype(F32)
    total = own_sum[...]
    aggregate = (total / divisor).astype(BF16)
    v = self_pre[...] + mm(aggregate, wn[...])
    root = math.sqrt(2.0 / math.pi)
    t = jnp.tanh(root * (v + 0.044715 * (v * v * v)))
    slope = 0.5 * (1.0 + t) + (0.5 * root) * v * (1.0 - t * t) * (1.0 + 0.134145 * (v * v))
    pre_grad = (cot[...].astype(F32) * slope).astype(BF16)

    def ng_copy(k, h):
        return remote(ngs.at[h, c], ngs.at[h, c], ng_sems, k * H + h, col_to(k))

    for h in range(H):
        ngs[h, c] = (mm(pre_grad, wn[parts[h], :], ((1,), (1,))) / divisor).astype(BF16)
        each(1, C, lambda k: ng_copy(k, h).start())
    act_out[...] = (0.5 * v * (1.0 + t)).astype(BF16)
    agg_ref[...] = aggregate
    pre_ref[...] = pre_grad
    if m:
        for half, operand in enumerate((feat, agg_ref)):
            grads = mm(operand[...], pre_ref[...], ((0,), (0,))) * inv_root
            for local in range(D // m):
                d = half * (D // m) + local
                rd, cd, pd = d // (2 * C), d // 2 % C, d % 2
                piece = grads[local * m : (local + 1) * m].astype(BF16)
                gw_send[pd, cd, rd * m : (rd + 1) * m] = piece
        gw_copy = remote(gw_send.at[q], gw_sib, sib_sems, 1, sib)
        gw_copy.start()
    else:
        gw_out[:D] = mm(feat[...], pre_ref[...], ((0,), (0,))) * inv_root
        gw_out[D:] = mm(agg_ref[...], pre_ref[...], ((0,), (0,))) * inv_root
    sp_own[...] = mm(pre_ref[...], ws[...], ((1,), (1,)))

    def spread_to(row, rep, h):
        block = row * 2 + rep
        slab = ngs[h].reshape(C * T, W)
        lines = pl.ds(pl.multiple_of(block * T, T), T)
        if inner:
            return mm(turned[lines, :], slab)
        return mm(asib[:, lines], slab, ((0,), (0,)))

    def gw1_copy(k):
        return remote(gw1_send.at[k], gw1_recv.at[k], gw1_sems, k, col_to(k))

    def gw2_copy(k):
        return remote(gw2_send.at[k], gw2_recv.at[k], gw2_sems, k, row_to(k))

    def sps_copy(k, h):
        return remote(sp_sib_send.at[h, k], sp_sib_recv.at[h, k], sps_sems, k * H + h, sib)

    def sp_copy(k, h):
        return remote(sp_sib_recv.at[h, k], sp_recv.at[h, k], sp_sems, k * H + h, row_to(k))

    for h in range(H):
        each(1, C, lambda k: ng_copy(k, h).wait_recv())

        def send_sib(k):
            sp_sib_send[h, k] = spread_to(lax.rem(r + k, R), q, h).astype(BF16)
            sps_copy(k, h).start()

        each(1, R, send_sib)
        send_sib(0)

        def send_spread(k):
            part = spread_to(lax.rem(r + k, R), p, h)
            sps_copy(k, h).wait_recv()
            sp_sib_recv[h, k] = (part + sp_sib_recv[h, k].astype(F32)).astype(BF16)
            sp_copy(k, h).start()

        each(1, R, send_spread)
        if m and h == 0:
            gw_copy.wait()

            def gw_part(block):
                return gw_send[p, block].astype(F32) + gw_sib[block].astype(F32)

            for k in range(1, C):
                gw1_send[k] = gw_part(lax.rem(c + k, C)).astype(BF16)
                gw1_copy(k).start()

    for h in range(H):
        part = spread_to(r, p, h)
        sps_copy(0, h).wait_recv()
        sp_own[:, parts[h]] += part + sp_sib_recv[h, 0].astype(F32)
    if m:
        weights = gw_part(c)
        for k in range(1, C):
            gw1_copy(k).wait_recv()
            weights = weights + gw1_recv[k].astype(F32)
        gw_tot[...] = weights

        def gw_rows(row):
            return gw_tot[pl.ds(pl.multiple_of(row * m, m), m), :]

        for k in range(1, R):
            gw2_send[k] = gw_rows(lax.rem(r + k, R)).astype(BF16)
            gw2_copy(k).start()

    for h in range(H):

        def add_spread(k):
            sp_copy(k, h).wait_recv()
            sp_own[:, parts[h]] += sp_recv[h, k].astype(F32)

        each(1, R, add_spread)
    gf_out[...] = sp_own[...].astype(BF16)
    if m:
        weights = gw_rows(r)
        for k in range(1, R):
            gw2_copy(k).wait_recv()
            weights = weights + gw2_recv[k].astype(F32)
        gw_out[...] = weights
        each(1, C, lambda k: gw1_copy(k).wait_send())
        each(1, R, lambda k: gw2_copy(k).wait_send())
    each(1, C, lambda k: deg_copy(k).wait_send())
    for h in range(H):
        each(1, R, lambda k: feat_copy(k, h).wait_send())
        each(1, R, lambda k: fwd_copy(k, h).wait_send())
        fwd_copy(0, h).wait_send()
        each(1, C, lambda k: sum_copy(k, h).wait_send())
        each(1, C, lambda k: ng_copy(k, h).wait_send())
        each(0, R, lambda k: sps_copy(k, h).wait_send())
        each(1, R, lambda k: sp_copy(k, h).wait_send())


def copy_kernel(a, b, c, to_a, to_b, to_c):
    to_a[...] = a[...]
    to_b[...] = b[...]
    to_c[...] = c[...]


def shards(features, w_self, w_neigh, cotangent, tile_row, tile_col, tile_mask, tile_count):
    R, C = lax.axis_size("row"), lax.axis_size("col")
    ndev = R * C * 2
    T, D = features.shape
    m = 2 * D // ndev
    fused = m % 16 == 0
    m = m if fused else 0
    inv_root = 1.0 / math.sqrt(T * ndev)
    slots = tile_row.shape[0]
    inner = R * C <= 16
    if inner:
        adjacency = tile_mask.reshape(slots * T, T)
    else:
        adjacency = build_adjacency(tile_row, tile_col, tile_count, tile_mask, C * 2, R * 2)
        adjacency = adjacency.reshape(2, C * T, R * 2 * T)
    V = pltpu.VMEM
    rows = max(m, 16)
    wr = rows * R if fused else 16
    dma = lambda n: pltpu.SemaphoreType.DMA((2, n))
    vm, hbm = pl.BlockSpec(memory_space=V), pl.BlockSpec(memory_space=pl.ANY)
    results = pl.pallas_call(
        functools.partial(layer_kernel, R, C, m, inv_root, inner),
        out_shape=(
            jax.ShapeDtypeStruct((T, D), BF16),
            jax.ShapeDtypeStruct((T, D), BF16),
            jax.ShapeDtypeStruct((m if fused else 2 * D, D), F32),
        ),
        in_specs=[hbm, vm, vm, vm, vm, hbm, hbm, vm],
        out_specs=(pl.BlockSpec(memory_space=V),) * 3,
        scratch_shapes=[
            V((slots * T, T) if inner else (8, T), jnp.int32),
            V((2 * R, 2 * C * T, T) if inner else (1, 8, T), F32),
            V((2, C * T, R * 2 * T), BF16),
            V((R * 2 * T, C * T) if inner else (16, T), BF16),
            V((D, D), BF16),
            V((D, D), BF16),
            pltpu.SemaphoreType.DMA((3,)),
            V((C * T, R * 2 * T), BF16),
            V((H, R * 2, T, D // H), BF16),
            V((C, 8, T), F32),
            V((C, 8, T), F32),
            V((H, C, T, D // H), BF16),
            V((H, C, T, D // H), BF16),
            V((T, D), F32),
            V((T, D), F32),
            V((T, D), BF16),
            V((T, D), BF16),
            V((H, C, T, D // H), BF16),
            V((H, R, T, D // H), BF16),
            V((H, R, T, D // H), BF16),
            V((H, R, T, D // H), BF16),
            V((T, D), F32),
            V((2, C, wr, D), BF16),
            V((C, wr, D), BF16),
            V((C, wr, D), BF16),
            V((C, wr, D), BF16),
            V((wr, D), F32),
            V((R, rows, D), BF16),
            V((R, rows, D), BF16),
            dma(2), dma(R * H), dma(R * H), dma(C), dma(C * H), dma(C * H), dma(R * H), dma(R * H),
            dma(C), dma(R),
        ],
        compiler_params=pltpu.CompilerParams(
            collective_id=0, has_side_effects=True, vmem_limit_bytes=60 * 2**20
        ),
    )(
        adjacency,
        tile_row.reshape(1, slots),
        tile_col.reshape(1, slots),
        tile_count.reshape(1, 1),
        features,
        w_self,
        w_neigh,
        cotangent,
    )
    activated, grad_features, grads = pl.pallas_call(
        copy_kernel,
        out_shape=tuple(jax.ShapeDtypeStruct(x.shape, x.dtype) for x in results),
        in_specs=[vm] * 3,
        out_specs=(vm,) * 3,
    )(*results)
    if not fused:
        grads = lax.psum_scatter(grads, ("row", "col", "rep"), scatter_dimension=0, tiled=True)
    return (activated, grad_features, grads)


def solution(mesh):
    placed = (
        P(("row", "col", "rep"), None),
        P(),
        P(),
        P(("row", "col", "rep"), None),
        P(("row", "col", "rep")),
        P(("row", "col", "rep")),
        P(("row", "col", "rep"), None, None),
        P(("row", "col", "rep")),
    )
    return jax.shard_map(
        shards,
        mesh=mesh,
        in_specs=placed,
        out_specs=(
            P(("row", "col", "rep"), None),
            P(("row", "col", "rep"), None),
            P(("row", "col", "rep"), None),
        ),
        check_vma=False,
    )
```

```python
import functools
import math

import jax
import jax.numpy as jnp
from jax import lax
from jax.experimental import pallas as pl
from jax.experimental.pallas import tpu as pltpu
from jax.sharding import PartitionSpec as P


def build_kernel(group, tile, row_blocks, rows_ref, cols_ref, count_ref, mask_ref, adj_ref):
    step = pl.program_id(0)

    @pl.when(step == 0)
    def _():
        adj_ref[...] = jnp.zeros_like(adj_ref)

    for lane in range(group):
        slot = step * group + lane

        @pl.when(slot < count_ref[0])
        def _():
            dest = rows_ref[slot]
            place = dest % 2 * (row_blocks // 2) + dest // 2
            row = pl.multiple_of(place * tile, tile)
            col = pl.multiple_of(cols_ref[slot] * tile, tile)
            where = (pl.ds(row, tile), pl.ds(col, tile))
            adj_ref[where] += mask_ref[lane].astype(jnp.float32).astype(jnp.bfloat16)


def build_adjacency(tile_row, tile_col, tile_count, tile_mask, row_blocks, col_blocks):
    slots, tile, _ = tile_mask.shape
    group = math.gcd(slots, 8)
    shape = (row_blocks * tile, col_blocks * tile)
    return pl.pallas_call(
        lambda *refs: build_kernel(group, tile, row_blocks, *refs),
        out_shape=jax.ShapeDtypeStruct(shape, jnp.bfloat16),
        grid_spec=pltpu.PrefetchScalarGridSpec(
            num_scalar_prefetch=3,
            grid=(slots // group,),
            in_specs=[pl.BlockSpec((group, tile, tile), lambda step, *_: (step, 0, 0))],
            out_specs=pl.BlockSpec(shape, lambda step, *_: (0, 0)),
        ),
        compiler_params=pltpu.CompilerParams(vmem_limit_bytes=48 * 2**20),
        cost_estimate=pl.CostEstimate(
            flops=slots * tile * tile, bytes_accessed=slots * tile * tile * 4, transcendentals=0
        ),
    )(tile_row, tile_col, tile_count, tile_mask)


MESH = pl.DeviceIdType.MESH
F32 = jnp.float32
BF16 = jnp.bfloat16
H = 2


def each(start, stop, body):
    if stop - start <= 8:
        for k in range(start, stop):
            body(k)
    else:

        def step(k, carry):
            body(k)
            return carry

        lax.fori_loop(start, stop, step, 0)


def mm(a, b, dims=((1,), (0,))):
    return lax.dot_general(a, b, (dims, ((), ())), preferred_element_type=F32)


def layer_kernel(
    R, C, m, inv_root, inner, adj_hbm, row_ids, col_ids, count, feat, ws_hbm, wn_hbm, cot,
    act_out, gf_out, gw_out, *scratch
):
    (
        tiles, wide, adj, turned, ws, wn, load_sems,
        asib, xg, deg_send, deg_recv, sum_send, sum_recv, own_sum, self_pre, agg_ref, pre_ref,
        ngs, sp_sib_send, sp_sib_recv, sp_recv, sp_own, gw_send, gw_sib, gw1_send,
        gw1_recv, gw_tot, gw2_send, gw2_recv, sib_sems, row_sems, fwd_sems, deg_sems, sum_sems,
        ng_sems, sps_sems, sp_sems, gw1_sems, gw2_sems,
    ) = scratch
    T, D = feat.shape
    W = D // H
    parts = [slice(h * W, (h + 1) * W) for h in range(H)]
    r, c, p = lax.axis_index("row"), lax.axis_index("col"), lax.axis_index("rep")
    q = 1 - p
    ws_load = pltpu.make_async_copy(ws_hbm, ws, load_sems.at[0])
    wn_load = pltpu.make_async_copy(wn_hbm, wn, load_sems.at[1])
    adj_load = pltpu.make_async_copy(adj_hbm, tiles if inner else adj, load_sems.at[2])
    adj_load.start()
    ws_load.start()
    wn_load.start()
    barrier = pltpu.get_barrier_semaphore()
    pl.semaphore_signal(barrier, inc=1, device_id={"rep": q}, device_id_type=MESH)
    each(1, R, lambda k: pl.semaphore_signal(
        barrier, inc=1, device_id={"row": lax.rem(r + k, R)}, device_id_type=MESH))
    each(1, C, lambda k: pl.semaphore_signal(
        barrier, inc=1, device_id={"col": lax.rem(c + k, C)}, device_id_type=MESH))
    pl.semaphore_wait(barrier, R + C - 1)

    def remote(src, dst, sems, k, target):
        return pltpu.make_async_remote_copy(
            src_ref=src, dst_ref=dst, send_sem=sems.at[0, k], recv_sem=sems.at[1, k],
            device_id=target, device_id_type=MESH)

    def row_to(k):
        return {"row": lax.rem(r + k, R)}

    def col_to(k):
        return {"col": lax.rem(c + k, C)}

    sib = {"rep": q}
    mine = r * 2 + p

    def feat_copy(k, h):
        source = feat.at[:, parts[h]]
        return remote(source, xg.at[h, mine], row_sems, k * H + h, row_to(k))

    def fwd_copy(k, h):
        block = lax.rem(r + R - k, R) * 2 + p
        own = isinstance(k, int) and k == 0
        source = feat.at[:, parts[h]] if own else xg.at[h, block]
        return remote(source, xg.at[h, block], fwd_sems, k * H + h, sib)

    for h in range(H):
        each(1, R, lambda k: feat_copy(k, h).start())
    for h in range(H):
        fwd_copy(0, h).start()
    adj_load.wait()
    if inner:
        slots = row_ids.shape[1]
        dest = row_ids[...]
        place = (dest & 1) * C + (dest >> 1)
        blocks = col_ids[...] * (2 * C) + place
        live = lax.broadcasted_iota(jnp.int32, (1, slots), 1) < count[...]
        blocks = jnp.where(live, blocks, -1)
        total_blocks = 4 * C * R
        pick = jnp.where(
            lax.broadcasted_iota(jnp.int32, (total_blocks, slots), 0) == blocks, 1.0, 0.0
        ).astype(BF16)

        def place_line(i, carry):
            lines = [
                tiles[pl.ds(2 * i + e, slots, stride=T), :].astype(F32).astype(BF16)
                for e in range(2)
            ]
            found = mm(pick, jnp.concatenate(lines, axis=1))
            for e in range(2):
                for j in range(2 * R):
                    wide[j, pl.ds(2 * i + e, 2 * C, stride=T), :] = found[
                        j * 2 * C : (j + 1) * 2 * C, e * T : (e + 1) * T
                    ]
            return carry

        lax.fori_loop(0, T // 2, place_line, 0, unroll=8)

    def narrow(half):
        half_rows = pl.ds(pl.multiple_of(half * (C * T), C * T), C * T)
        for j in range(2 * R):
            adj[half, :, j * T : (j + 1) * T] = wide[j, half_rows, :].astype(BF16)

    if inner:
        narrow(q)
    adj_copy = remote(adj.at[q], asib, sib_sems, 0, sib)
    adj_copy.start()
    if inner:
        narrow(p)
    for h in range(H):
        xg[h, mine] = feat[:, parts[h]]
    ws_load.wait()
    wn_load.wait()
    self_pre[...] = mm(feat[...], ws[...])

    def forward(k, h):
        feat_copy(k, h).wait_recv()
        fwd_copy(k, h).start()

    each(1, R, lambda k: forward(k, 0))
    adj_copy.wait()
    asib[...] += adj[p]

    def rows_of(block):
        return asib[pl.ds(pl.multiple_of(block * T, T), T), :]

    def sum_copy(k, h):
        return remote(sum_send.at[h, k], sum_recv.at[h, k], sum_sems, k * H + h, col_to(k))

    for h in range(H):
        if h > 0:
            each(1, R, lambda k: forward(k, h))
        each(0, R, lambda k: fwd_copy(k, h).wait_recv())
        sources = xg[h].reshape(R * 2 * T, W)

        def send_sum(k):
            sum_send[h, k] = mm(rows_of(lax.rem(c + k, C)), sources).astype(BF16)
            sum_copy(k, h).start()

        each(1, C, send_sum)
        own_sum[:, parts[h]] = mm(rows_of(c), sources)
    ones = jnp.ones((8, asib.shape[1]), BF16)

    def deg_copy(k):
        return remote(deg_send.at[k], deg_recv.at[k], deg_sems, k, col_to(k))

    def send_degree(k):
        deg_send[k] = mm(ones, rows_of(lax.rem(c + k, C)), ((1,), (1,)))
        deg_copy(k).start()

    each(1, C, send_degree)
    degree = mm(ones, rows_of(c), ((1,), (1,)))

    if inner:
        turned[...] = asib[...].T

    for k in range(1, C):
        deg_copy(k).wait_recv()
        degree = degree + deg_recv[k]
    diagonal = lax.broadcasted_iota(jnp.int32, (T, T), 0) == lax.broadcasted_iota(
        jnp.int32, (T, T), 1)
    spread_degree = jnp.broadcast_to(degree[0:1, :], (T, T))
    divisor = jnp.sum(jnp.where(diagonal, spread_degree, 0.0), axis=1, keepdims=True) + 1.0
    for h in range(H):
        for k in range(1, C):
            sum_copy(k, h).wait_recv()
            own_sum[:, parts[h]] += sum_recv[h, k].astype(F32)
    total = own_sum[...]
    aggregate = (total / divisor).astype(BF16)
    v = self_pre[...] + mm(aggregate, wn[...])
    root = math.sqrt(2.0 / math.pi)
    t = jnp.tanh(root * (v + 0.044715 * (v * v * v)))
    slope = 0.5 * (1.0 + t) + (0.5 * root) * v * (1.0 - t * t) * (1.0 + 0.134145 * (v * v))
    pre_grad = (cot[...].astype(F32) * slope).astype(BF16)

    def ng_copy(k, h):
        return remote(ngs.at[h, c], ngs.at[h, c], ng_sems, k * H + h, col_to(k))

    for h in range(H):
        ngs[h, c] = (mm(pre_grad, wn[parts[h], :], ((1,), (1,))) / divisor).astype(BF16)
        each(1, C, lambda k: ng_copy(k, h).start())
    act_out[...] = (0.5 * v * (1.0 + t)).astype(BF16)
    agg_ref[...] = aggregate
    pre_ref[...] = pre_grad
    if m:
        for half, operand in enumerate((feat, agg_ref)):
            grads = mm(operand[...], pre_ref[...], ((0,), (0,))) * inv_root
            for local in range(D // m):
                d = half * (D // m) + local
                rd, cd, pd = d // (2 * C), d // 2 % C, d % 2
                piece = grads[local * m : (local + 1) * m].astype(BF16)
                gw_send[pd, cd, rd * m : (rd + 1) * m] = piece
        gw_copy = remote(gw_send.at[q], gw_sib, sib_sems, 1, sib)
        gw_copy.start()
    else:
        gw_out[:D] = mm(feat[...], pre_ref[...], ((0,), (0,))) * inv_root
        gw_out[D:] = mm(agg_ref[...], pre_ref[...], ((0,), (0,))) * inv_root
    sp_own[...] = mm(pre_ref[...], ws[...], ((1,), (1,)))

    def spread_to(row, rep, h):
        block = row * 2 + rep
        slab = ngs[h].reshape(C * T, W)
        lines = pl.ds(pl.multiple_of(block * T, T), T)
        if inner:
            return mm(turned[lines, :], slab)
        return mm(asib[:, lines], slab, ((0,), (0,)))

    def gw1_copy(k):
        return remote(gw1_send.at[k], gw1_recv.at[k], gw1_sems, k, col_to(k))

    def gw2_copy(k):
        return remote(gw2_send.at[k], gw2_recv.at[k], gw2_sems, k, row_to(k))

    def sps_copy(k, h):
        return remote(sp_sib_send.at[h, k], sp_sib_recv.at[h, k], sps_sems, k * H + h, sib)

    def sp_copy(k, h):
        return remote(sp_sib_recv.at[h, k], sp_recv.at[h, k], sp_sems, k * H + h, row_to(k))

    for h in range(H):
        each(1, C, lambda k: ng_copy(k, h).wait_recv())

        def send_sib(k):
            sp_sib_send[h, k] = spread_to(lax.rem(r + k, R), q, h).astype(BF16)
            sps_copy(k, h).start()

        each(1, R, send_sib)
        send_sib(0)

        def send_spread(k):
            part = spread_to(lax.rem(r + k, R), p, h)
            sps_copy(k, h).wait_recv()
            sp_sib_recv[h, k] = (part + sp_sib_recv[h, k].astype(F32)).astype(BF16)
            sp_copy(k, h).start()

        each(1, R, send_spread)
        if m and h == 0:
            gw_copy.wait()

            def gw_part(block):
                return gw_send[p, block].astype(F32) + gw_sib[block].astype(F32)

            for k in range(1, C):
                gw1_send[k] = gw_part(lax.rem(c + k, C)).astype(BF16)
                gw1_copy(k).start()

    for h in range(H):
        part = spread_to(r, p, h)
        sps_copy(0, h).wait_recv()
        sp_own[:, parts[h]] += part + sp_sib_recv[h, 0].astype(F32)
    if m:
        weights = gw_part(c)
        for k in range(1, C):
            gw1_copy(k).wait_recv()
            weights = weights + gw1_recv[k].astype(F32)
        gw_tot[...] = weights

        def gw_rows(row):
            return gw_tot[pl.ds(pl.multiple_of(row * m, m), m), :]

        for k in range(1, R):
            gw2_send[k] = gw_rows(lax.rem(r + k, R)).astype(BF16)
            gw2_copy(k).start()

    for h in range(H):

        def add_spread(k):
            sp_copy(k, h).wait_recv()
            sp_own[:, parts[h]] += sp_recv[h, k].astype(F32)

        each(1, R, add_spread)
    gf_out[...] = sp_own[...].astype(BF16)
    if m:
        weights = gw_rows(r)
        for k in range(1, R):
            gw2_copy(k).wait_recv()
            weights = weights + gw2_recv[k].astype(F32)
        gw_out[...] = weights
        each(1, C, lambda k: gw1_copy(k).wait_send())
        each(1, R, lambda k: gw2_copy(k).wait_send())
    each(1, C, lambda k: deg_copy(k).wait_send())
    for h in range(H):
        each(1, R, lambda k: feat_copy(k, h).wait_send())
        each(1, R, lambda k: fwd_copy(k, h).wait_send())
        fwd_copy(0, h).wait_send()
        each(1, C, lambda k: sum_copy(k, h).wait_send())
        each(1, C, lambda k: ng_copy(k, h).wait_send())
        each(0, R, lambda k: sps_copy(k, h).wait_send())
        each(1, R, lambda k: sp_copy(k, h).wait_send())


def copy_kernel(a, b, c, to_a, to_b, to_c):
    to_a[...] = a[...]
    to_b[...] = b[...]
    to_c[...] = c[...]


def shards(features, w_self, w_neigh, cotangent, tile_row, tile_col, tile_mask, tile_count):
    R, C = lax.axis_size("row"), lax.axis_size("col")
    ndev = R * C * 2
    T, D = features.shape
    m = 2 * D // ndev
    fused = m % 16 == 0
    m = m if fused else 0
    inv_root = 1.0 / math.sqrt(T * ndev)
    slots = tile_row.shape[0]
    inner = R * C <= 16
    if inner:
        adjacency = tile_mask.reshape(slots * T, T)
    else:
        adjacency = build_adjacency(tile_row, tile_col, tile_count, tile_mask, C * 2, R * 2)
        adjacency = adjacency.reshape(2, C * T, R * 2 * T)
    V = pltpu.VMEM
    rows = max(m, 16)
    wr = rows * R if fused else 16
    dma = lambda n: pltpu.SemaphoreType.DMA((2, n))
    vm, hbm = pl.BlockSpec(memory_space=V), pl.BlockSpec(memory_space=pl.ANY)
    results = pl.pallas_call(
        functools.partial(layer_kernel, R, C, m, inv_root, inner),
        out_shape=(
            jax.ShapeDtypeStruct((T, D), BF16),
            jax.ShapeDtypeStruct((T, D), BF16),
            jax.ShapeDtypeStruct((m if fused else 2 * D, D), F32),
        ),
        in_specs=[hbm, vm, vm, vm, vm, hbm, hbm, vm],
        out_specs=(pl.BlockSpec(memory_space=V),) * 3,
        scratch_shapes=[
            V((slots * T, T) if inner else (8, T), jnp.int32),
            V((2 * R, 2 * C * T, T) if inner else (1, 8, T), F32),
            V((2, C * T, R * 2 * T), BF16),
            V((R * 2 * T, C * T) if inner else (16, T), BF16),
            V((D, D), BF16),
            V((D, D), BF16),
            pltpu.SemaphoreType.DMA((3,)),
            V((C * T, R * 2 * T), BF16),
            V((H, R * 2, T, D // H), BF16),
            V((C, 8, T), F32),
            V((C, 8, T), F32),
            V((H, C, T, D // H), BF16),
            V((H, C, T, D // H), BF16),
            V((T, D), F32),
            V((T, D), F32),
            V((T, D), BF16),
            V((T, D), BF16),
            V((H, C, T, D // H), BF16),
            V((H, R, T, D // H), BF16),
            V((H, R, T, D // H), BF16),
            V((H, R, T, D // H), BF16),
            V((T, D), F32),
            V((2, C, wr, D), BF16),
            V((C, wr, D), BF16),
            V((C, wr, D), BF16),
            V((C, wr, D), BF16),
            V((wr, D), F32),
            V((R, rows, D), BF16),
            V((R, rows, D), BF16),
            dma(2), dma(R * H), dma(R * H), dma(C), dma(C * H), dma(C * H), dma(R * H), dma(R * H),
            dma(C), dma(R),
        ],
        compiler_params=pltpu.CompilerParams(
            collective_id=0, has_side_effects=True, vmem_limit_bytes=60 * 2**20
        ),
    )(
        adjacency,
        tile_row.reshape(1, slots),
        tile_col.reshape(1, slots),
        tile_count.reshape(1, 1),
        features,
        w_self,
        w_neigh,
        cotangent,
    )
    activated, grad_features, grads = pl.pallas_call(
        copy_kernel,
        out_shape=tuple(jax.ShapeDtypeStruct(x.shape, x.dtype) for x in results),
        in_specs=[vm] * 3,
        out_specs=(vm,) * 3,
    )(*results)
    if not fused:
        grads = lax.psum_scatter(grads, ("row", "col", "rep"), scatter_dimension=0, tiled=True)
    return (activated, grad_features, grads)


def solution(mesh):
    placed = (
        P(("row", "col", "rep"), None),
        P(),
        P(),
        P(("row", "col", "rep"), None),
        P(("row", "col", "rep")),
        P(("row", "col", "rep")),
        P(("row", "col", "rep"), None, None),
        P(("row", "col", "rep")),
    )
    return jax.shard_map(
        shards,
        mesh=mesh,
        in_specs=placed,
        out_specs=(
            P(("row", "col", "rep"), None),
            P(("row", "col", "rep"), None),
            P(("row", "col", "rep"), None),
        ),
        check_vma=False,
    )
```
